32 devices in a mesh: loop: 8 (over y, x, core), tp: 4 (over z).
Axes of the slice: x: 2, y: 2, z: 4, core: 2. Of those that a mesh axis runs over, the one named last changes fastest.
Arguments:
- tokens: bfloat16 [2048, 4096], P('loop', 'tp'), may hold values from -6 to 6
- out_grad: bfloat16 [2048, 6144], P('loop', 'tp'), may hold values from -6 to 6
- qkv_weight: bfloat16 [3, 4096, 6144], P(None, 'loop', 'tp'), may hold values from -0.09375 to 0.09375
- dest_row: int32 [2048], P('loop'), may hold values from 0 to 383, as said below
- loop_modality: int32 [8], replicated, may hold values from 0 to 2, as said below
Outputs:
- projected: bfloat16 [2048, 6144], P('loop', 'tp')
- input_grad: bfloat16 [2048, 4096], P('loop', 'tp')
- weight_grad: bfloat16 [3, 4096, 6144], P(None, 'loop', 'tp')
The draws below stay inside these ranges and needn't reach their ends.
Inputs may be any that keep to these rules, and one draw needn't show every extreme that they name: `dest_row`: within each aligned block of 256 tokens the values are distinct, so at most 48 tokens of one block name one loop; in every draw some loop is named by exactly 48 tokens of every block. `loop_modality`: A quarter of the loops hold 0, half hold 1, a quarter hold 2.
All inputs are finite; a program needn't handle non-finite values.
Results may differ from the reference program's by a relative error of at most 0.014.
Values may be sent and summed in bfloat16 or wider, within the bound.
No kernel may reach another device: no remote copies, remote signals or barrier semaphores. Data moves between devices by JAX's collectives and lax.ppermute only.
A program may use at most 128 MiB of HBM per device.

```python
import jax
import jax.numpy as jnp
from jax import lax

D = 4096
MODALITIES = 3
TOK_LOOP = 256
QKV = 6144
CAP = 48
TOKENS = 2048
N_LOOP = 8
N_TP = 4


def draw_loop_modality(key, part):
    shuffle = jax.random.permutation(key, N_LOOP)
    return jnp.where(shuffle < N_LOOP // 4, 0, jnp.where(shuffle < 3 * N_LOOP // 4, 1, 2)).astype(jnp.int32)


def draw_dest_row(key, part):
    slot_count = N_LOOP * CAP
    full_key = jax.random.fold_in(key, 7)
    bias_key = jax.random.fold_in(key, 11)
    target = jax.random.randint(full_key, (), 0, N_LOOP)
    loop_bias = jax.random.randint(bias_key, (N_LOOP,), 0, 32768)
    slot_ids = jnp.arange(slot_count, dtype=jnp.int32)
    slot_owner = slot_ids // CAP

    def one_source(source_index):
        source_key = jax.random.fold_in(key, 1000 + source_index)
        jitter = jax.random.randint(jax.random.fold_in(source_key, 1), (slot_count,), 0, 32768)
        priority = jitter + loop_bias[slot_owner] + jnp.where(slot_owner == target, 131072, 0) + jnp.where(slot_ids == slot_count - 1, 65536, 0)
        priority = priority * 8192 + slot_ids
        _, chosen = lax.top_k(priority, TOK_LOOP)
        shuffle = jax.random.permutation(jax.random.fold_in(source_key, 2), TOK_LOOP)
        return chosen[shuffle].astype(jnp.int32)
    return jax.vmap(one_source)(jnp.arange(N_LOOP, dtype=jnp.int32)).reshape(-1).astype(jnp.int32)


def block_scale(own_key, shape, cuts, smallest, largest):
    level = 1.0
    for axis_at, parts in cuts:
        heights = jax.random.uniform(jax.random.fold_in(jax.random.fold_in(own_key, 6), axis_at), (parts,), jnp.float32, smallest / len(cuts), largest / len(cuts))
        level = level * jnp.repeat(jnp.exp(heights), shape[axis_at] // parts).reshape((-1,) + (1,) * (len(shape) - 1 - axis_at))
    return level


def normal_values(key, dims, spread, reach, cuts=(), kind=jnp.bfloat16):
    drawn = spread * jax.random.normal(key, dims, jnp.float32)
    if cuts:
        drawn = drawn * block_scale(key, dims, cuts, -0.22, 0.18)
    return jnp.clip(drawn, -reach, reach).astype(kind)


def setup_inputs(seed: int = 0) -> dict:
    keys = jax.random.split(jax.random.key(seed), 6)
    tokens = normal_values(keys[0], (TOKENS, D), 1.0, 6.0, ((0, 8), (1, 4)))
    out_grad = normal_values(keys[1], (TOKENS, QKV), 1.0, 6.0, ((0, 8), (1, 4)))
    qkv_weight = normal_values(keys[2], (MODALITIES, D, QKV), D ** -0.5, 0.09375, ((1, 8), (2, 4)))
    dest_row = draw_dest_row(jax.random.fold_in(keys[5], 71), 0)
    loop_modality = draw_loop_modality(jax.random.fold_in(keys[5], 71), 0)
    return dict(tokens=tokens, out_grad=out_grad, qkv_weight=qkv_weight, dest_row=dest_row, loop_modality=loop_modality)


def reference(tokens, out_grad, qkv_weight, dest_row, loop_modality):
    slot_count = N_LOOP * CAP
    source = (jnp.arange(TOKENS, dtype=jnp.int32) // TOK_LOOP).astype(jnp.int32)
    target = (dest_row // CAP).astype(jnp.int32)
    position_index = (target * slot_count + source * CAP + dest_row % CAP).astype(jnp.int32)
    token_buffer = jnp.zeros((N_LOOP * slot_count, D), jnp.bfloat16).at[position_index].set(tokens)
    token_buffer = token_buffer.reshape(N_LOOP, slot_count, D)
    grad_buffer = jnp.zeros((N_LOOP * slot_count, QKV), jnp.bfloat16).at[position_index].set(out_grad)
    grad_buffer = grad_buffer.reshape(N_LOOP, slot_count, QKV)
    group_width = QKV // N_TP
    grad_scale = float(TOKENS) ** -0.5

    def loop_step(accumulated, loop_item):
        token_rows, grad_rows, modality = loop_item
        weight = lax.dynamic_index_in_dim(qkv_weight, modality, 0, keepdims=False)
        projected = jnp.dot(token_rows, weight, preferred_element_type=jnp.float32).astype(jnp.bfloat16)
        summed = jnp.zeros((slot_count, D), jnp.float32)
        for group_index in range(N_TP):
            lower = group_index * group_width
            group_term = lax.dot_general(grad_rows[:, lower:lower + group_width], weight[:, lower:lower + group_width], (((1,), (1,)), ((), ())), preferred_element_type=jnp.float32)
            rounded = lax.optimization_barrier(group_term.astype(jnp.bfloat16))
            summed = summed + rounded.astype(jnp.float32)
        weight_part = lax.dot_general(token_rows, grad_rows, (((0,), (0,)), ((), ())), preferred_element_type=jnp.float32) * grad_scale
        accumulated = accumulated.at[modality].add(weight_part)
        return accumulated, (projected, summed.astype(jnp.bfloat16))

    initial = jnp.zeros((MODALITIES, D, QKV), jnp.float32)
    accumulated, (outputs, input_grads) = lax.scan(loop_step, initial, (token_buffer, grad_buffer, loop_modality))
    projected_rows = outputs.reshape(N_LOOP * slot_count, QKV)[position_index]
    input_grad = input_grads.reshape(N_LOOP * slot_count, D)[position_index]
    return projected_rows, input_grad, accumulated.astype(jnp.bfloat16)
```

```python
import math

import jax
import jax.numpy as jnp
from jax import lax
from jax.sharding import PartitionSpec as P


def per_device(tokens, out_grad, qkv_weight, dest_row, loop_modality):
    loop_count = lax.axis_size("loop")
    row_count, feature_part = tokens.shape
    kinds, block_rows, column_count = qkv_weight.shape
    capacity = 3 * row_count // (2 * loop_count)
    grad_scale = 1.0 / math.sqrt(row_count * loop_count)
    own_kind = loop_modality[dest_row // capacity]
    kind_of = lax.all_gather(own_kind, "loop", axis=0, tiled=True)
    grads = lax.all_gather(out_grad, "loop", axis=0, tiled=True)
    features = lax.all_gather(tokens, "tp", axis=1, tiled=True)
    rows = lax.all_to_all(features, "loop", split_axis=1, concat_axis=0, tiled=True)
    masks = [(kind_of == kind)[:, None] for kind in range(kinds)]
    term = sum(
        lax.dot_general(
            jnp.where(masks[kind], grads, 0), qkv_weight[kind], (((1,), (1,)), ((), ())),
            preferred_element_type=jnp.float32,
        )
        for kind in range(kinds)
    ).astype(jnp.bfloat16)
    term = lax.all_to_all(term, "loop", split_axis=0, concat_axis=1, tiled=True)
    input_grad = lax.psum_scatter(term, "tp", scatter_dimension=1, tiled=True)
    partial = sum(
        jnp.dot(jnp.where(masks[kind], rows, 0), qkv_weight[kind], preferred_element_type=jnp.float32)
        for kind in range(kinds)
    ).astype(jnp.bfloat16)
    projected = lax.psum_scatter(partial, "loop", scatter_dimension=0, tiled=True)
    weight_grad = jnp.stack([
        (
            lax.dot_general(
                jnp.where(masks[kind], rows, 0), grads, (((0,), (0,)), ((), ())),
                preferred_element_type=jnp.float32,
            )
            * grad_scale
        ).astype(jnp.bfloat16)
        for kind in range(kinds)
    ])
    return projected, input_grad, weight_grad


def solution(mesh):
    placed = (P("loop", "tp"), P("loop", "tp"), P(None, "loop", "tp"), P("loop"), P())
    return jax.shard_map(
        per_device,
        mesh=mesh,
        in_specs=placed,
        out_specs=(P("loop", "tp"), P("loop", "tp"), P(None, "loop", "tp")),
        check_vma=False,
    )
```

```python
import functools
import math

import jax
import jax.numpy as jnp
from jax import lax
from jax.experimental import pallas as pl
from jax.experimental.pallas import tpu as pltpu
from jax.sharding import PartitionSpec as P

BF16 = jnp.bfloat16
F32 = jnp.float32


def kind_kernel(kinds_of_loops, dest, out, *, capacity):
    slots = dest[...]
    found = jnp.full(slots.shape, kinds_of_loops[0], jnp.int32)
    for loop_index in range(1, kinds_of_loops.shape[0]):
        found = jnp.where(slots >= loop_index * capacity, kinds_of_loops[loop_index], found)
    out[...] = found


def modality_of(dest_row, loop_modality, capacity):
    slots = dest_row.reshape(1, -1)
    return pl.pallas_call(
        functools.partial(kind_kernel, capacity=capacity),
        out_shape=jax.ShapeDtypeStruct(slots.shape, jnp.int32),
        in_specs=[pl.BlockSpec(memory_space=pltpu.SMEM), pl.BlockSpec(memory_space=pltpu.VMEM)],
        out_specs=pl.BlockSpec(memory_space=pltpu.VMEM),
    )(loop_modality, slots)


def pick(kind, products):
    chosen = products[0]
    for index in range(1, len(products)):
        chosen = jnp.where(kind == index, products[index], chosen)
    return chosen


def whole(shape):
    return pl.BlockSpec(shape, lambda *_: (0,) * len(shape))


def split_rows(value, outs):
    start = 0
    for out in outs:
        yield out, value[start:start + out.shape[0]]
        start += out.shape[0]


def input_kernel(core, kind, own_weight, other_weight, *refs, count, tile):
    lhs = jnp.concatenate([ref[...] for ref in refs[:count]], axis=0)
    outs = refs[count:]
    half = outs[0].shape[1] // 2
    for weight, side in ((own_weight, core[0]), (other_weight, 1 - core[0])):
        products = [
            lax.dot_general(lhs, weight[index], (((1,), (1,)), ((), ())), preferred_element_type=F32)
            for index in range(weight.shape[0])
        ]
        chosen = pick(kind[...], products).astype(BF16)
        at = pl.multiple_of(side * half + pl.program_id(0) * tile, tile)
        for out, part in split_rows(chosen, outs):
            out[:, pl.ds(at, tile)] = part


def input_terms(core, kind, blocks, own_weight, other_weight):
    kinds, half, columns = own_weight.shape
    tile = min(half, 256)
    weight_spec = pl.BlockSpec((kinds, tile, columns), lambda step, core: (0, step, 0))
    return pl.pallas_call(
        functools.partial(input_kernel, count=len(blocks), tile=tile),
        grid_spec=pltpu.PrefetchScalarGridSpec(
            num_scalar_prefetch=1,
            grid=(half // tile,),
            in_specs=[whole(kind.shape), weight_spec, weight_spec] + [whole(block.shape) for block in blocks],
            out_specs=[whole((block.shape[0], 2 * half)) for block in blocks],
        ),
        out_shape=[jax.ShapeDtypeStruct((block.shape[0], 2 * half), BF16) for block in blocks],
    )(core, kind, own_weight, other_weight, *blocks)


def project_kernel(core, kind, own_weight, other_weight, *refs, count):
    half = own_weight.shape[1]
    own_at = pl.multiple_of(core[0] * half, half)
    other_at = pl.multiple_of((1 - core[0]) * half, half)
    own = jnp.concatenate([ref[:, pl.ds(own_at, half)] for ref in refs[:count]], axis=0)
    other = jnp.concatenate([ref[:, pl.ds(other_at, half)] for ref in refs[:count]], axis=0)
    products = [
        jnp.dot(own, own_weight[index], preferred_element_type=F32)
        + jnp.dot(other, other_weight[index], preferred_element_type=F32)
        for index in range(own_weight.shape[0])
    ]
    chosen = pick(kind[...], products).astype(BF16)
    for out, part in split_rows(chosen, refs[count:]):
        out[...] = part


def project_parts(core, kind, blocks, own_weight, other_weight):
    kinds, half, columns = own_weight.shape
    tile = min(columns, 256)
    weight_spec = pl.BlockSpec((kinds, half, tile), lambda step, core: (0, 0, step))
    return pl.pallas_call(
        functools.partial(project_kernel, count=len(blocks)),
        grid_spec=pltpu.PrefetchScalarGridSpec(
            num_scalar_prefetch=1,
            grid=(columns // tile,),
            in_specs=[whole(kind.shape), weight_spec, weight_spec] + [whole(block.shape) for block in blocks],
            out_specs=[
                pl.BlockSpec((block.shape[0], tile), lambda step, core: (0, step)) for block in blocks
            ],
        ),
        out_shape=[jax.ShapeDtypeStruct((block.shape[0], columns), BF16) for block in blocks],
    )(core, kind, own_weight, other_weight, *blocks)


def weight_kernel(core, kind, *refs, near, far, grads, scale):
    rows = refs[:near + far]
    cotangents = refs[near + far:near + far + grads]
    out, turned = refs[near + far + grads:]
    kinds, half, _ = out.shape

    @pl.when(pl.program_id(0) == 0)
    def _():
        start = 0
        for index, ref in enumerate(rows):
            count = ref.shape[0]
            part = ref[:, pl.ds(pl.multiple_of(core[0] * half, half), half)] if index < near else ref[...]
            part = part.T
            own_kind = kind[:, start:start + count]
            for which in range(kinds):
                turned[which, :, start:start + count] = jnp.where(own_kind == which, part, 0)
            start += count

    columns = jnp.concatenate([ref[...] for ref in cotangents], axis=0)
    for which in range(kinds):
        total = jnp.dot(turned[which], columns, preferred_element_type=F32)
        out[which] = (total * scale).astype(BF16)


def weight_gradient(core, kind, near, far, grads, kinds, scale):
    half = far[0].shape[1]
    columns = grads[0].shape[1]
    tile = min(columns, 256)
    rows = kind.shape[1]
    return pl.pallas_call(
        functools.partial(weight_kernel, near=len(near), far=len(far), grads=len(grads), scale=scale),
        grid_spec=pltpu.PrefetchScalarGridSpec(
            num_scalar_prefetch=1,
            grid=(columns // tile,),
            in_specs=[whole(kind.shape)]
            + [whole(block.shape) for block in (*near, *far)]
            + [pl.BlockSpec((block.shape[0], tile), lambda step, core: (0, step)) for block in grads],
            out_specs=pl.BlockSpec((kinds, half, tile), lambda step, core: (0, 0, step)),
            scratch_shapes=[pltpu.VMEM((kinds, half, rows), BF16)],
        ),
        out_shape=jax.ShapeDtypeStruct((kinds, half, columns), BF16),
    )(core, kind, *near, *far, *grads)


def per_device(tokens, out_grad, qkv_weight, dest_row, loop_modality):
    loop_count = lax.axis_size("loop")
    tp_count = lax.axis_size("tp")
    row_count, feature_part = tokens.shape
    kinds, half, column_count = qkv_weight.shape
    chip_count = loop_count // 2
    assert chip_count == tp_count and 2 * half == feature_part
    capacity = 3 * row_count // (2 * loop_count)
    grad_scale = 1.0 / math.sqrt(row_count * loop_count)
    loop_index = lax.axis_index("loop")
    chip, level = loop_index // 2, lax.axis_index("tp")
    core = (loop_index % 2).astype(jnp.int32).reshape(1)
    bits = [1 << place for place in range(chip_count.bit_length() - 1)]

    def across(value, offset):
        return lax.ppermute(value, "loop", [(i, i ^ (2 * offset)) for i in range(loop_count)])

    def sibling(value):
        return lax.ppermute(value, "loop", [(i, i ^ 1) for i in range(loop_count)])

    def shift(value, step):
        pairs = [(i, i + step) for i in range(tp_count) if 0 <= i + step < tp_count]
        return lax.ppermute(value, "tp", pairs)

    def low_high(offset):
        return offset & -offset, 1 << (offset.bit_length() - 1)

    offsets = sorted(range(1, chip_count), key=lambda offset: (bin(offset).count("1"), offset))
    several = [offset for offset in offsets if offset & (offset - 1)]

    rising, falling = [tokens], [tokens]
    for _ in range(tp_count - 1):
        rising.append(shift(rising[-1], 1))
        falling.append(shift(falling[-1], -1))

    grads = {0: [out_grad]}
    for offset in offsets:
        if offset in bits:
            grads[offset] = [across(out_grad, offset)]
        else:
            low, high = low_high(offset)
            first = jnp.concatenate(grads[offset ^ low], axis=0)[:row_count // 2]
            second = jnp.concatenate(grads[offset ^ high], axis=0)[row_count // 2:]
            grads[offset] = [across(first, low), across(second, high)]

    own_kind = modality_of(dest_row, loop_modality, capacity)
    kind = own_kind
    for bit in bits:
        kind = jnp.concatenate([kind, across(kind, bit)], axis=0)
    other_kind = sibling(kind)
    other_weight = sibling(qkv_weight)
    kind_rows = kind[:, :, None]

    arrived = {}
    for group in ([offset for offset in offsets if offset in bits], several, [0]):
        blocks = [block for offset in group for block in grads[offset]]
        group_kind = jnp.concatenate([kind_rows[offset] for offset in group], axis=0)
        made = input_terms(core, group_kind, blocks, qkv_weight, other_weight)
        at = 0
        for offset in group:
            mine = made[at:at + len(grads[offset])]
            at += len(grads[offset])
            term = mine[0] if len(mine) == 1 else jnp.concatenate(mine, axis=0)
            arrived[offset] = across(term, offset) if offset else term
    terms = jnp.stack([arrived[offset] for offset in range(chip_count)])

    def level_term(where):
        return lax.dynamic_index_in_dim(terms, chip ^ jnp.clip(where, 0, tp_count - 1), 0, keepdims=False)

    up = down = None
    for step in range(1, tp_count):
        up_send = level_term(tp_count - step + level)
        down_send = level_term(level - tp_count + step)
        if up is not None:
            up_send = (up_send.astype(F32) + up.astype(F32)).astype(BF16)
            down_send = (down_send.astype(F32) + down.astype(F32)).astype(BF16)
        up, down = shift(up_send, 1), shift(down_send, -1)
    input_grad = (level_term(level).astype(F32) + up.astype(F32) + down.astype(F32)).astype(BF16)

    levels = jnp.stack(
        [tokens]
        + [jnp.where(level >= step, rising[step], falling[tp_count - step]) for step in range(1, tp_count)]
    )

    def level_tokens(where):
        return lax.dynamic_index_in_dim(levels, (level - where) % tp_count, 0, keepdims=False)

    rows = {
        offset: across(level_tokens(chip ^ offset), offset) if offset else level_tokens(chip)
        for offset in range(chip_count)
    }

    parts = {}
    for group in (several, [offset for offset in offsets if offset in bits] + [0]):
        group_kind = jnp.concatenate([kind_rows[offset] for offset in group], axis=0)
        made = project_parts(core, group_kind, [rows[offset] for offset in group], qkv_weight, other_weight)
        for offset, part in zip(group, made):
            parts[offset] = [part[:row_count // 2], part[row_count // 2:]] if group is several else part
    pieces = {offset: [] for offset in range(chip_count)}

    def add_pieces(offset, halves):
        halves = [half_part.astype(F32) for half_part in halves]
        for place, piece in pieces[offset]:
            halves[place] = halves[place] + piece.astype(F32)
        return [half_part.astype(BF16) for half_part in halves]

    for offset in reversed(several):
        low, high = low_high(offset)
        first, second = add_pieces(offset, parts[offset])
        pieces[offset ^ low].append((0, across(first, low)))
        pieces[offset ^ high].append((1, across(second, high)))
    for offset in bits:
        parts[offset] = jnp.concatenate(add_pieces(offset, jnp.split(parts[offset], 2, axis=0)), axis=0)
    total = parts[0].astype(F32)
    for offset in bits:
        total = total + across(parts[offset], offset).astype(F32)
    projected = total.astype(BF16)

    near = [rows[offset] for offset in range(chip_count)]
    side = (1 - core[0]) * half
    far = [sibling(lax.dynamic_slice_in_dim(block, side, half, axis=1)) for block in near]
    near_grads = [block for offset in range(chip_count) for block in grads[offset]]
    far_grads = [sibling(block) for block in near_grads]
    all_kind = jnp.concatenate([kind.reshape(1, -1), other_kind.reshape(1, -1)], axis=1)
    weight_grad = weight_gradient(core, all_kind, near, far, near_grads + far_grads, kinds, grad_scale)
    return projected, input_grad, weight_grad


def solution(mesh):
    placed = (P("loop", "tp"), P("loop", "tp"), P(None, "loop", "tp"), P("loop"), P())
    return jax.shard_map(
        per_device,
        mesh=mesh,
        in_specs=placed,
        out_specs=(P("loop", "tp"), P("loop", "tp"), P(None, "loop", "tp")),
        check_vma=False,
    )
```

```python
import functools
import math

import jax
import jax.numpy as jnp
from jax import lax
from jax.experimental import pallas as pl
from jax.experimental.pallas import tpu as pltpu
from jax.sharding import PartitionSpec as P


BF16 = jnp.bfloat16
F32 = jnp.float32


def kind_kernel(kinds_of_loops, dest, out, *, capacity):
    slots = dest[...]
    found = jnp.full(slots.shape, kinds_of_loops[0], jnp.int32)
    for loop_index in range(1, kinds_of_loops.shape[0]):
        found = jnp.where(slots >= loop_index * capacity, kinds_of_loops[loop_index], found)
    out[...] = found


def modality_of(dest_row, loop_modality, capacity):
    slots = dest_row.reshape(1, -1)
    return pl.pallas_call(
        functools.partial(kind_kernel, capacity=capacity),
        out_shape=jax.ShapeDtypeStruct(slots.shape, jnp.int32),
        in_specs=[pl.BlockSpec(memory_space=pltpu.SMEM), pl.BlockSpec(memory_space=pltpu.VMEM)],
        out_specs=pl.BlockSpec(memory_space=pltpu.VMEM),
    )(loop_modality, slots)


def pick(kind, products):
    chosen = products[0]
    for index in range(1, len(products)):
        chosen = jnp.where(kind == index, products[index], chosen)
    return chosen


def whole(shape):
    return pl.BlockSpec(shape, lambda *_: (0,) * len(shape))


def split_rows(value, outs):
    start = 0
    for out in outs:
        yield out, value[start:start + out.shape[0]]
        start += out.shape[0]


def limit(mebibytes):
    return pltpu.CompilerParams(vmem_limit_bytes=mebibytes << 20)


def input_kernel(core, kind, own_weight, other_weight, *refs, blocks, tile):
    rhs = jnp.concatenate([ref[...] for ref in refs[:blocks]], axis=0)
    outs = refs[blocks:]
    half = outs[0].shape[1] // 2
    kinds, _, columns = own_weight.shape
    for weight, side in ((own_weight, core[0]), (other_weight, 1 - core[0])):
        product = lax.dot_general(
            weight[...].reshape(kinds * tile, columns), rhs, (((1,), (1,)), ((), ())),
            preferred_element_type=F32,
        )
        products = [product[index * tile:(index + 1) * tile] for index in range(kinds)]
        chosen = pick(kind[...], products).astype(BF16).T
        at = pl.multiple_of(side * half + pl.program_id(0) * tile, tile)
        for out, part in split_rows(chosen, outs):
            out[:, pl.ds(at, tile)] = part


def input_terms(core, kind, blocks, sizes, own_weight, other_weight):
    kinds, half, columns = own_weight.shape
    tile = min(half, 256)
    weight_spec = pl.BlockSpec((kinds, tile, columns), lambda step, core: (0, step, 0))
    return pl.pallas_call(
        functools.partial(input_kernel, blocks=len(blocks), tile=tile),
        grid_spec=pltpu.PrefetchScalarGridSpec(
            num_scalar_prefetch=1,
            grid=(half // tile,),
            in_specs=[whole(kind.shape), weight_spec, weight_spec] + [whole(block.shape) for block in blocks],
            out_specs=[whole((size, 2 * half)) for size in sizes],
        ),
        out_shape=[jax.ShapeDtypeStruct((size, 2 * half), BF16) for size in sizes],
        compiler_params=limit(28),
    )(core, kind, own_weight, other_weight, *blocks)


def project_kernel(core, kind, own_weight, other_weight, *refs, blocks):
    _, half, tile = own_weight.shape
    own_at = pl.multiple_of(core[0] * half, half)
    other_at = pl.multiple_of((1 - core[0]) * half, half)
    own = jnp.concatenate([ref[:, pl.ds(own_at, half)] for ref in refs[:blocks]], axis=0)
    other = jnp.concatenate([ref[:, pl.ds(other_at, half)] for ref in refs[:blocks]], axis=0)
    row_kind = jnp.broadcast_to(kind[...], (tile, own.shape[0])).T
    products = [
        jnp.dot(own, own_weight[index], preferred_element_type=F32)
        + jnp.dot(other, other_weight[index], preferred_element_type=F32)
        for index in range(own_weight.shape[0])
    ]
    chosen = pick(row_kind, products).astype(BF16)
    for out, part in split_rows(chosen, refs[blocks:]):
        out[...] = part


def project_parts(core, kind, blocks, sizes, own_weight, other_weight):
    kinds, half, columns = own_weight.shape
    tile = math.gcd(columns, 512)
    weight_spec = pl.BlockSpec((kinds, half, tile), lambda step, core: (0, 0, step))
    return pl.pallas_call(
        functools.partial(project_kernel, blocks=len(blocks)),
        grid_spec=pltpu.PrefetchScalarGridSpec(
            num_scalar_prefetch=1,
            grid=(columns // tile,),
            in_specs=[whole(kind.shape), weight_spec, weight_spec] + [whole(block.shape) for block in blocks],
            out_specs=[pl.BlockSpec((size, tile), lambda step, core: (0, step)) for size in sizes],
        ),
        out_shape=[jax.ShapeDtypeStruct((size, columns), BF16) for size in sizes],
        compiler_params=limit(28),
    )(core, kind, own_weight, other_weight, *blocks)


def choose_kernel(wanted, *refs, sources):
    outs = refs[sources:]
    for place, out in enumerate(outs):
        for index, source in enumerate(refs[:sources]):
            @pl.when(wanted[place] == index)
            def _(out=out, source=source):
                out[...] = source[...]


def choose(wanted, sources, count):
    rows, columns = sources[0].shape
    step_rows = rows // 4
    spec = pl.BlockSpec((step_rows, columns), lambda step, wanted: (step, 0))
    return pl.pallas_call(
        functools.partial(choose_kernel, sources=len(sources)),
        grid_spec=pltpu.PrefetchScalarGridSpec(
            num_scalar_prefetch=1,
            grid=(4,),
            in_specs=[spec] * len(sources),
            out_specs=[spec] * count,
        ),
        out_shape=[jax.ShapeDtypeStruct((rows, columns), sources[0].dtype)] * count,
        compiler_params=limit(16),
    )(wanted, *sources)


def weight_kernel(core, kind, *refs, blocks, grads, scale):
    rows = refs[:blocks]
    cotangents = refs[blocks:blocks + grads]
    out, turned = refs[blocks + grads:]
    kinds, half, _ = out.shape

    @pl.when(pl.program_id(0) == 0)
    def _():
        start = 0
        for ref in rows:
            count = ref.shape[0]
            part = ref[:, pl.ds(pl.multiple_of(core[0] * half, half), half)].T
            own_kind = kind[:, start:start + count]
            for which in range(kinds):
                turned[which, :, start:start + count] = jnp.where(own_kind == which, part, 0)
            start += count

    columns = jnp.concatenate([ref[...] for ref in cotangents], axis=0)
    for which in range(kinds):
        total = jnp.dot(turned[which], columns, preferred_element_type=F32)
        out[which] = (total * scale).astype(BF16)


def weight_gradient(core, kind, blocks, grads, kinds, scale):
    half = blocks[0].shape[1] // 2
    columns = grads[0].shape[1]
    tile = min(columns, 256)
    rows = kind.shape[1]
    return pl.pallas_call(
        functools.partial(weight_kernel, blocks=len(blocks), grads=len(grads), scale=scale),
        grid_spec=pltpu.PrefetchScalarGridSpec(
            num_scalar_prefetch=1,
            grid=(columns // tile,),
            in_specs=[whole(kind.shape)]
            + [whole(block.shape) for block in blocks]
            + [pl.BlockSpec((block.shape[0], tile), lambda step, core: (0, step)) for block in grads],
            out_specs=pl.BlockSpec((kinds, half, tile), lambda step, core: (0, 0, step)),
            scratch_shapes=[pltpu.VMEM((kinds, half, rows), BF16)],
        ),
        out_shape=jax.ShapeDtypeStruct((kinds, half, columns), BF16),
        compiler_params=limit(36),
    )(core, kind, *blocks, *grads)


def low_high(offset):
    return offset & -offset, 1 << (offset.bit_length() - 1)


def body(tokens, out_grad, qkv_weight, dest_row, loop_modality):
    loop_count = lax.axis_size("loop")
    tp_count = lax.axis_size("tp")
    row_count, feature_part = tokens.shape
    kinds, half, _ = qkv_weight.shape
    chip_count = loop_count // 2
    assert chip_count == tp_count and 2 * half == feature_part
    capacity = 3 * row_count // (2 * loop_count)
    grad_scale = 1.0 / math.sqrt(row_count * loop_count)
    loop_index = lax.axis_index("loop")
    chip, level = loop_index >> 1, lax.axis_index("tp")
    core = (loop_index & 1).reshape(1)
    bits = [1 << place for place in range(chip_count.bit_length() - 1)]
    offsets = sorted(range(1, chip_count), key=lambda offset: (bin(offset).count("1"), offset))
    several = [offset for offset in offsets if offset & (offset - 1)]
    cut = row_count // 2

    def across(value, offset):
        pairs = [(i, i ^ (2 * offset)) for i in range(loop_count)]
        return lax.ppermute(value, "loop", pairs)

    def sibling(value):
        return lax.ppermute(value, "loop", [(i, i ^ 1) for i in range(loop_count)])

    def line_pairs(parity, stage):
        pairs = []
        for low in range(parity, tp_count - 1, 2):
            if low - stage + 1 >= 0:
                pairs.append((low, low + 1))
            if low + stage <= tp_count - 1:
                pairs.append((low + 1, low))
        return pairs

    def along(value, pairs):
        return lax.ppermute(value, "tp", pairs)

    stages = range(1, tp_count)
    facing = [jnp.where(level % 2 == parity, 1, -1) for parity in (0, 1)]

    other_weight = sibling(qkv_weight)
    came = {(0, 0): tokens, (1, 0): tokens}
    for stage in stages:
        for parity in (0, 1):
            pairs = line_pairs(parity, stage)
            if pairs:
                came[parity, stage] = along(came[1 - parity, stage - 1], pairs)

    own_grad = [out_grad[:cut], out_grad[cut:]]
    grads = {0: own_grad}
    for bit in bits:
        grads[bit] = [None, None]
    for bit in bits:
        first = 0 if bit == bits[-1] else 1
        for part in (first, 1 - first):
            grads[bit][part] = across(own_grad[part], bit)
    for offset in several:
        low, high = low_high(offset)
        grads[offset] = [across(grads[offset ^ low][0], low), across(grads[offset ^ high][1], high)]

    own_kind = modality_of(dest_row, loop_modality, capacity)
    kind = own_kind
    for bit in bits:
        kind = jnp.concatenate([kind, across(kind, bit)], axis=0)
    other_kind = sibling(kind)
    kind_of = [own_kind] + [kind[offset:offset + 1] for offset in range(1, chip_count)]

    def group_kind(group):
        return jnp.concatenate([kind_of[offset] for offset in group], axis=1)

    arrived = {}
    for group in ([0], bits, several):
        blocks = [out_grad] if group == [0] else [part for offset in group for part in grads[offset]]
        made = input_terms(core, group_kind(group), blocks, [row_count] * len(group), qkv_weight, other_weight)
        for offset, term in zip(group, made):
            arrived[offset] = across(term, offset) if offset else term
    all_terms = [arrived[offset] for offset in range(chip_count)]

    def level_term(where):
        offset = chip ^ jnp.clip(where, 0, tp_count - 1)
        term = all_terms[0]
        for index in range(1, chip_count):
            term = jnp.where(offset == index, all_terms[index], term)
        return term.astype(F32)

    back = {}
    for stage in reversed(stages):
        for parity in (0, 1):
            pairs = line_pairs(parity, stage)
            if pairs:
                value = level_term(level + stage * facing[parity])
                if (1 - parity, stage + 1) in back:
                    value = value + back[1 - parity, stage + 1].astype(F32)
                back[parity, stage] = along(value.astype(BF16), [(b, a) for a, b in pairs])
    input_grad = level_term(level)
    for parity in (0, 1):
        if (parity, 1) in back:
            input_grad = input_grad + back[parity, 1].astype(F32)
    input_grad = input_grad.astype(BF16)

    places = [place for place in came if place != (1, 0)]
    sources = [came[place] for place in places]
    wanted = []
    for offset in range(chip_count):
        where = chip ^ offset
        index = jnp.int32(0)
        for number, (parity, stage) in enumerate(places):
            if stage:
                index = jnp.where(where == level + stage * facing[parity], number, index)
        wanted.append(index)
    sends = choose(jnp.stack(wanted), sources, chip_count)
    rows = {offset: across(sends[offset], offset) if offset else sends[offset] for offset in range(chip_count)}

    parts = {}
    for group in (several, bits + [0]):
        made = project_parts(
            core, group_kind(group), [rows[offset] for offset in group],
            [cut] * (2 * len(group)), qkv_weight, other_weight,
        )
        for place, offset in enumerate(group):
            parts[offset] = [part.astype(F32) for part in made[2 * place:2 * place + 2]]
    for offset in reversed(several):
        low, high = low_high(offset)
        for part, (near, link) in enumerate(((offset ^ low, low), (offset ^ high, high))):
            piece = across(parts[offset][part].astype(BF16), link)
            parts[near][part] = parts[near][part] + piece.astype(F32)
    for bit in bits:
        for part in (0, 1):
            piece = across(parts[bit][part].astype(BF16), bit)
            parts[0][part] = parts[0][part] + piece.astype(F32)
    projected = jnp.concatenate([part.astype(BF16) for part in parts[0]], axis=0)

    near = [rows[offset] for offset in range(chip_count)]
    far = [sibling(block) for block in near]
    near_grads = [out_grad] + [part for offset in range(1, chip_count) for part in grads[offset]]
    far_grads = [sibling(block) for block in near_grads]
    all_kind = jnp.concatenate([kind.reshape(1, -1), other_kind.reshape(1, -1)], axis=1)
    weight_grad = weight_gradient(core, all_kind, near + far, near_grads + far_grads, kinds, grad_scale)
    return projected, input_grad, weight_grad


def solution(mesh):
    placed = (P("loop", "tp"), P("loop", "tp"), P(None, "loop", "tp"), P("loop"), P())
    return jax.shard_map(
        body,
        mesh=mesh,
        in_specs=placed,
        out_specs=(P("loop", "tp"), P("loop", "tp"), P(None, "loop", "tp")),
        check_vma=False,
    )
```

```python
import functools
import math

import jax
import jax.numpy as jnp
from jax import lax
from jax.experimental import pallas as pl
from jax.experimental.pallas import tpu as pltpu
from jax.sharding import PartitionSpec as P


BF16 = jnp.bfloat16
F32 = jnp.float32
KIND_ROWS = 8
PROJECT_TILE = 512
WEIGHT_TILE = 256


def pack_kernel(kinds_of_loops, dest, grads, *outs, capacity):
    slots = dest[...]
    found = jnp.full(slots.shape, kinds_of_loops[0], jnp.int32)
    for loop_index in range(1, kinds_of_loops.shape[0]):
        found = jnp.where(slots >= loop_index * capacity, kinds_of_loops[loop_index], found)
    cut = slots.shape[1] // len(outs)
    for part, out in enumerate(outs):
        extra = out.shape[0] - cut
        kind = found[:, part * cut:(part + 1) * cut].astype(F32).astype(BF16)
        out[:cut] = grads[part * cut:(part + 1) * cut]
        out[cut:] = jnp.zeros((extra, out.shape[1]), BF16)
        out[cut:, :cut] = jnp.broadcast_to(kind, (extra, cut))


def packed_grads(out_grad, dest_row, loop_modality, capacity):
    rows, columns = out_grad.shape
    slots = dest_row.reshape(1, -1)
    vmem = pl.BlockSpec(memory_space=pltpu.VMEM)
    return pl.pallas_call(
        functools.partial(pack_kernel, capacity=capacity),
        out_shape=[jax.ShapeDtypeStruct((rows // 2 + KIND_ROWS, columns), BF16)] * 2,
        in_specs=[pl.BlockSpec(memory_space=pltpu.SMEM), vmem, vmem],
        out_specs=[vmem, vmem],
        compiler_params=limit(8),
    )(loop_modality, slots, out_grad)


def kinds_in(refs):
    return jnp.concatenate([ref[:1].astype(F32) for ref in refs], axis=1)


def kind_spec(half_block):
    cut = half_block.shape[0] - KIND_ROWS
    return pl.BlockSpec((KIND_ROWS, cut), lambda *_: (cut // KIND_ROWS, 0))


def pick(kind, products):
    chosen = products[0]
    for index in range(1, len(products)):
        chosen = jnp.where(kind == index, products[index], chosen)
    return chosen


def whole(shape):
    return pl.BlockSpec(shape, lambda *_: (0,) * len(shape))


def split_rows(value, outs):
    start = 0
    for out in outs:
        yield out, value[start:start + out.shape[0]]
        start += out.shape[0]


def limit(mebibytes):
    return pltpu.CompilerParams(vmem_limit_bytes=mebibytes << 20)


def input_kernel(core, own_weight, other_weight, *refs, blocks, tile):
    cut = refs[0].shape[0] - KIND_ROWS
    rhs = jnp.concatenate([ref[:cut] for ref in refs[:blocks]], axis=0)
    kind = kinds_in([ref[cut:, :cut] for ref in refs[:blocks]])
    outs = refs[blocks:]
    half = outs[0].shape[1] // 2
    kinds, _, columns = own_weight.shape
    for weight, side in ((own_weight, core[0]), (other_weight, 1 - core[0])):
        product = lax.dot_general(
            weight[...].reshape(kinds * tile, columns), rhs, (((1,), (1,)), ((), ())),
            preferred_element_type=F32,
        )
        products = [product[index * tile:(index + 1) * tile] for index in range(kinds)]
        chosen = pick(kind, products).astype(BF16).T
        at = pl.multiple_of(side * half + pl.program_id(0) * tile, tile)
        for out, part in split_rows(chosen, outs):
            out[:, pl.ds(at, tile)] = part


def input_terms(core, blocks, sizes, own_weight, other_weight):
    kinds, half, columns = own_weight.shape
    tile = min(half, 256)
    weight_spec = pl.BlockSpec((kinds, tile, columns), lambda step, core: (0, step, 0))
    return pl.pallas_call(
        functools.partial(input_kernel, blocks=len(blocks), tile=tile),
        grid_spec=pltpu.PrefetchScalarGridSpec(
            num_scalar_prefetch=1,
            grid=(half // tile,),
            in_specs=[weight_spec, weight_spec] + [whole(block.shape) for block in blocks],
            out_specs=[whole((size, 2 * half)) for size in sizes],
        ),
        out_shape=[jax.ShapeDtypeStruct((size, 2 * half), BF16) for size in sizes],
        compiler_params=limit(28),
    )(core, own_weight, other_weight, *blocks)


def project_kernel(core, own_weight, other_weight, *refs, blocks, halves):
    _, half, tile = own_weight.shape
    own_at = pl.multiple_of(core[0] * half, half)
    other_at = pl.multiple_of((1 - core[0]) * half, half)
    own = jnp.concatenate([ref[:, pl.ds(own_at, half)] for ref in refs[:blocks]], axis=0)
    other = jnp.concatenate([ref[:, pl.ds(other_at, half)] for ref in refs[:blocks]], axis=0)
    kind = kinds_in([ref[...] for ref in refs[blocks:blocks + halves]])
    row_kind = jnp.broadcast_to(kind, (tile, kind.shape[1])).T
    products = [
        jnp.dot(own, own_weight[index], preferred_element_type=F32)
        + jnp.dot(other, other_weight[index], preferred_element_type=F32)
        for index in range(own_weight.shape[0])
    ]
    chosen = pick(row_kind, products).astype(BF16)
    for out, part in split_rows(chosen, refs[blocks + halves:]):
        out[...] = part


def project_parts(core, blocks, half_blocks, sizes, own_weight, other_weight):
    kinds, half, columns = own_weight.shape
    tile = math.gcd(columns, PROJECT_TILE)
    weight_spec = pl.BlockSpec((kinds, half, tile), lambda step, core: (0, 0, step))
    return pl.pallas_call(
        functools.partial(project_kernel, blocks=len(blocks), halves=len(half_blocks)),
        grid_spec=pltpu.PrefetchScalarGridSpec(
            num_scalar_prefetch=1,
            grid=(columns // tile,),
            in_specs=[weight_spec, weight_spec]
            + [whole(block.shape) for block in blocks]
            + [kind_spec(block) for block in half_blocks],
            out_specs=[pl.BlockSpec((size, tile), lambda step, core: (0, step)) for size in sizes],
        ),
        out_shape=[jax.ShapeDtypeStruct((size, columns), BF16) for size in sizes],
        compiler_params=limit(28),
    )(core, own_weight, other_weight, *blocks, *half_blocks)


def choose_kernel(wanted, *refs, sources):
    outs, done = refs[sources:-1], refs[-1]
    for place, out in enumerate(outs):
        for index, source in enumerate(refs[:sources]):
            @pl.when(wanted[place] == index)
            def _(place=place, out=out, source=source):
                pltpu.make_async_copy(source, out, done.at[place]).start()
    for place, out in enumerate(outs):
        pltpu.make_async_copy(refs[0], out, done.at[place]).wait()


def choose(wanted, sources, count):
    any_space = pl.BlockSpec(memory_space=pl.ANY)
    return pl.pallas_call(
        functools.partial(choose_kernel, sources=len(sources)),
        in_specs=[pl.BlockSpec(memory_space=pltpu.SMEM)] + [any_space] * len(sources),
        out_specs=[any_space] * count,
        out_shape=[jax.ShapeDtypeStruct(sources[0].shape, sources[0].dtype)] * count,
        scratch_shapes=[pltpu.SemaphoreType.DMA((count,))],
        compiler_params=limit(4),
    )(wanted, *sources)


def weight_kernel(core, *refs, blocks, grads, scale):
    rows = refs[:blocks]
    columns_of = refs[blocks:blocks + grads]
    kind_rows = refs[blocks + grads:blocks + 2 * grads]
    out, turned = refs[blocks + 2 * grads:]
    kinds, half, _ = out.shape

    @pl.when(pl.program_id(0) == 0)
    def _():
        kind = kinds_in([ref[...] for ref in kind_rows])
        start = 0
        for ref in rows:
            count = ref.shape[0]
            part = ref[:, pl.ds(pl.multiple_of(core[0] * half, half), half)].T
            own_kind = kind[:, start:start + count]
            for which in range(kinds):
                turned[which, :, start:start + count] = jnp.where(own_kind == which, part, 0)
            start += count

    columns = jnp.concatenate([ref[...] for ref in columns_of], axis=0)
    for which in range(kinds):
        total = jnp.dot(turned[which], columns, preferred_element_type=F32)
        out[which] = (total * scale).astype(BF16)


def weight_gradient(core, blocks, half_blocks, kinds, scale):
    rows, features = blocks[0].shape
    half = features // 2
    columns = half_blocks[0].shape[1]
    cut = half_blocks[0].shape[0] - KIND_ROWS
    tile = math.gcd(columns, WEIGHT_TILE)
    return pl.pallas_call(
        functools.partial(weight_kernel, blocks=len(blocks), grads=len(half_blocks), scale=scale),
        grid_spec=pltpu.PrefetchScalarGridSpec(
            num_scalar_prefetch=1,
            grid=(columns // tile,),
            in_specs=[whole(block.shape) for block in blocks]
            + [pl.BlockSpec((cut, tile), lambda step, core: (0, step)) for _ in half_blocks]
            + [kind_spec(block) for block in half_blocks],
            out_specs=pl.BlockSpec((kinds, half, tile), lambda step, core: (0, 0, step)),
            scratch_shapes=[pltpu.VMEM((kinds, half, rows * len(blocks)), BF16)],
        ),
        out_shape=jax.ShapeDtypeStruct((kinds, half, columns), BF16),
        compiler_params=limit(36),
    )(core, *blocks, *half_blocks, *half_blocks)


def low_high(offset):
    return offset & -offset, 1 << (offset.bit_length() - 1)


def body(tokens, out_grad, qkv_weight, dest_row, loop_modality):
    loop_count = lax.axis_size("loop")
    tp_count = lax.axis_size("tp")
    row_count, feature_part = tokens.shape
    kinds, half, _ = qkv_weight.shape
    chip_count = loop_count // 2
    assert chip_count == tp_count and 2 * half == feature_part
    capacity = 3 * row_count // (2 * loop_count)
    grad_scale = 1.0 / math.sqrt(row_count * loop_count)
    loop_index = lax.axis_index("loop")
    chip, level = loop_index >> 1, lax.axis_index("tp")
    core = (loop_index & 1).reshape(1)
    bits = [1 << place for place in range(chip_count.bit_length() - 1)]
    offsets = sorted(range(1, chip_count), key=lambda offset: (bin(offset).count("1"), offset))
    several = [offset for offset in offsets if offset & (offset - 1)]
    cut = row_count // 2

    def across(value, offset):
        pairs = [(i, i ^ (2 * offset)) for i in range(loop_count)]
        return lax.ppermute(value, "loop", pairs)

    def sibling(value):
        return lax.ppermute(value, "loop", [(i, i ^ 1) for i in range(loop_count)])

    def line_pairs(parity, stage):
        pairs = []
        for low in range(parity, tp_count - 1, 2):
            if low - stage + 1 >= 0:
                pairs.append((low, low + 1))
            if low + stage <= tp_count - 1:
                pairs.append((low + 1, low))
        return pairs

    def along(value, pairs):
        return lax.ppermute(value, "tp", pairs)

    stages = range(1, tp_count)
    facing = [jnp.where(level % 2 == parity, 1, -1) for parity in (0, 1)]

    other_weight = sibling(qkv_weight)
    came = {(0, 0): tokens, (1, 0): tokens}
    for stage in stages:
        for parity in (0, 1):
            pairs = line_pairs(parity, stage)
            if pairs:
                came[parity, stage] = along(came[1 - parity, stage - 1], pairs)

    own_grad = packed_grads(out_grad, dest_row, loop_modality, capacity)
    grads = {0: own_grad}
    for bit in bits:
        grads[bit] = [None, None]
    for bit in bits:
        first = 0 if bit == bits[-1] else 1
        for part in (first, 1 - first):
            grads[bit][part] = across(own_grad[part], bit)
    for offset in several:
        low, high = low_high(offset)
        grads[offset] = [across(grads[offset ^ low][0], low), across(grads[offset ^ high][1], high)]

    def halves_of(group):
        return [part for offset in group for part in grads[offset]]

    arrived = {}
    for group in ([0], bits, several):
        made = input_terms(
            core, halves_of(group), [row_count] * len(group), qkv_weight, other_weight
        )
        for offset, term in zip(group, made):
            arrived[offset] = across(term, offset) if offset else term
    all_terms = [arrived[offset] for offset in range(chip_count)]

    def level_term(where):
        offset = chip ^ jnp.clip(where, 0, tp_count - 1)
        term = all_terms[0]
        for index in range(1, chip_count):
            term = jnp.where(offset == index, all_terms[index], term)
        return term.astype(F32)

    back = {}
    for stage in reversed(stages):
        for parity in (0, 1):
            pairs = line_pairs(parity, stage)
            if pairs:
                value = level_term(level + stage * facing[parity])
                if (1 - parity, stage + 1) in back:
                    value = value + back[1 - parity, stage + 1].astype(F32)
                back[parity, stage] = along(value.astype(BF16), [(b, a) for a, b in pairs])
    input_grad = level_term(level)
    for parity in (0, 1):
        if (parity, 1) in back:
            input_grad = input_grad + back[parity, 1].astype(F32)
    input_grad = input_grad.astype(BF16)

    places = [place for place in came if place != (1, 0)]
    sources = [came[place] for place in places]
    wanted = []
    for offset in range(chip_count):
        where = chip ^ offset
        index = jnp.int32(0)
        for number, (parity, stage) in enumerate(places):
            if stage:
                index = jnp.where(where == level + stage * facing[parity], number, index)
        wanted.append(index)
    sends = choose(jnp.stack(wanted), sources, chip_count)
    rows = {
        offset: across(sends[offset], offset) if offset else sends[offset]
        for offset in range(chip_count)
    }

    parts = {}
    for group in (several, bits, [0]):
        made = project_parts(
            core, [rows[offset] for offset in group], halves_of(group),
            [cut] * (2 * len(group)), qkv_weight, other_weight,
        )
        for place, offset in enumerate(group):
            parts[offset] = [part.astype(F32) for part in made[2 * place:2 * place + 2]]
    for offset in reversed(several):
        low, high = low_high(offset)
        for part, (near, link) in enumerate(((offset ^ low, low), (offset ^ high, high))):
            piece = across(parts[offset][part].astype(BF16), link)
            parts[near][part] = parts[near][part] + piece.astype(F32)
    for bit in bits:
        for part in (0, 1):
            piece = across(parts[bit][part].astype(BF16), bit)
            parts[0][part] = parts[0][part] + piece.astype(F32)
    projected = jnp.concatenate([part.astype(BF16) for part in parts[0]], axis=0)

    near = [rows[offset] for offset in range(chip_count)]
    far = [sibling(block) for block in near]
    near_grads = halves_of(range(chip_count))
    far_grads = [sibling(block) for block in near_grads]
    weight_grad = weight_gradient(core, near + far, near_grads + far_grads, kinds, grad_scale)
    return projected, input_grad, weight_grad


def solution(mesh):
    placed = (P("loop", "tp"), P("loop", "tp"), P(None, "loop", "tp"), P("loop"), P())
    return jax.shard_map(
        body,
        mesh=mesh,
        in_specs=placed,
        out_specs=(P("loop", "tp"), P("loop", "tp"), P(None, "loop", "tp")),
        check_vma=False,
    )
```

```python
import functools
import math

import jax
import jax.numpy as jnp
from jax import lax
from jax.experimental import pallas as pl
from jax.experimental.pallas import tpu as pltpu
from jax.sharding import PartitionSpec as P


BF16 = jnp.bfloat16
F32 = jnp.float32
KIND_ROWS = 8
PROJECT_TILE = 512
CHOOSE_STEPS = 2
WEIGHT_TILE = 512


def pack_kernel(kinds_of_loops, dest, grads, *outs, capacity):
    slots = dest[...]
    found = jnp.full(slots.shape, kinds_of_loops[0], jnp.int32)
    for loop_index in range(1, kinds_of_loops.shape[0]):
        found = jnp.where(slots >= loop_index * capacity, kinds_of_loops[loop_index], found)
    cut = slots.shape[1] // len(outs)
    for part, out in enumerate(outs):
        extra = out.shape[0] - cut
        kind = found[:, part * cut:(part + 1) * cut].astype(F32).astype(BF16)
        out[:cut] = grads[part * cut:(part + 1) * cut]
        out[cut:] = jnp.zeros((extra, out.shape[1]), BF16)
        out[cut:, :cut] = jnp.broadcast_to(kind, (extra, cut))


def packed_grads(out_grad, dest_row, loop_modality, capacity):
    rows, columns = out_grad.shape
    slots = dest_row.reshape(1, -1)
    packed = (rows // 2 + KIND_ROWS, columns)
    return pl.pallas_call(
        functools.partial(pack_kernel, capacity=capacity),
        grid_spec=pltpu.PrefetchScalarGridSpec(
            num_scalar_prefetch=1,
            grid=(1,),
            in_specs=[whole(slots.shape), whole(out_grad.shape)],
            out_specs=[whole(packed), whole(packed)],
        ),
        out_shape=[jax.ShapeDtypeStruct(packed, BF16)] * 2,
        compiler_params=limit(8),
    )(loop_modality, slots, out_grad)


def in_hbm(value):
    return pltpu.with_memory_space_constraint(value, pltpu.HBM)


def kinds_in(refs):
    return jnp.concatenate([ref[:1].astype(F32) for ref in refs], axis=1)


def kind_spec(half_block):
    cut = half_block.shape[0] - KIND_ROWS
    return pl.BlockSpec((KIND_ROWS, cut), lambda *_: (cut // KIND_ROWS, 0))


def pick(kind, products):
    chosen = products[0]
    for index in range(1, len(products)):
        chosen = jnp.where(kind == index, products[index], chosen)
    return chosen


def whole(shape):
    return pl.BlockSpec(shape, lambda *_: (0,) * len(shape))


def split_rows(value, outs):
    start = 0
    for out in outs:
        yield out, value[start:start + out.shape[0]]
        start += out.shape[0]


def limit(mebibytes):
    return pltpu.CompilerParams(vmem_limit_bytes=mebibytes << 20)


def input_kernel(core, own_weight, other_weight, *refs, blocks, tile):
    cut = refs[0].shape[0] - KIND_ROWS
    rhs = jnp.concatenate([ref[:cut] for ref in refs[:blocks]], axis=0)
    kind = kinds_in([ref[cut:, :cut] for ref in refs[:blocks]])
    outs = refs[blocks:]
    half = outs[0].shape[1] // 2
    kinds, _, columns = own_weight.shape
    for weight, side in ((own_weight, core[0]), (other_weight, 1 - core[0])):
        product = lax.dot_general(
            weight[...].reshape(kinds * tile, columns), rhs, (((1,), (1,)), ((), ())),
            preferred_element_type=F32,
        )
        products = [product[index * tile:(index + 1) * tile] for index in range(kinds)]
        chosen = pick(kind, products).astype(BF16).T
        at = pl.multiple_of(side * half + pl.program_id(0) * tile, tile)
        for out, part in split_rows(chosen, outs):
            out[:, pl.ds(at, tile)] = part


def input_terms(core, blocks, sizes, own_weight, other_weight):
    kinds, half, columns = own_weight.shape
    tile = min(half, 256)
    weight_spec = pl.BlockSpec((kinds, tile, columns), lambda step, core: (0, step, 0))
    return pl.pallas_call(
        functools.partial(input_kernel, blocks=len(blocks), tile=tile),
        grid_spec=pltpu.PrefetchScalarGridSpec(
            num_scalar_prefetch=1,
            grid=(half // tile,),
            in_specs=[weight_spec, weight_spec] + [whole(block.shape) for block in blocks],
            out_specs=[whole((size, 2 * half)) for size in sizes],
        ),
        out_shape=[jax.ShapeDtypeStruct((size, 2 * half), BF16) for size in sizes],
        compiler_params=limit(28),
    )(core, in_hbm(own_weight), in_hbm(other_weight), *blocks)


def project_kernel(core, own_weight, other_weight, *refs, blocks, halves):
    _, half, tile = own_weight.shape
    own_at = pl.multiple_of(core[0] * half, half)
    other_at = pl.multiple_of((1 - core[0]) * half, half)
    own = jnp.concatenate([ref[:, pl.ds(own_at, half)] for ref in refs[:blocks]], axis=0)
    other = jnp.concatenate([ref[:, pl.ds(other_at, half)] for ref in refs[:blocks]], axis=0)
    kind = kinds_in([ref[...] for ref in refs[blocks:blocks + halves]])
    row_kind = jnp.broadcast_to(kind, (tile, kind.shape[1])).T
    products = [
        jnp.dot(own, own_weight[index], preferred_element_type=F32)
        + jnp.dot(other, other_weight[index], preferred_element_type=F32)
        for index in range(own_weight.shape[0])
    ]
    chosen = pick(row_kind, products).astype(BF16)
    for out, part in split_rows(chosen, refs[blocks + halves:]):
        out[...] = part


def project_parts(core, blocks, half_blocks, sizes, own_weight, other_weight):
    kinds, half, columns = own_weight.shape
    tile = math.gcd(columns, PROJECT_TILE)
    weight_spec = pl.BlockSpec((kinds, half, tile), lambda step, core: (0, 0, step))
    return pl.pallas_call(
        functools.partial(project_kernel, blocks=len(blocks), halves=len(half_blocks)),
        grid_spec=pltpu.PrefetchScalarGridSpec(
            num_scalar_prefetch=1,
            grid=(columns // tile,),
            in_specs=[weight_spec, weight_spec]
            + [whole(block.shape) for block in blocks]
            + [kind_spec(block) for block in half_blocks],
            out_specs=[pl.BlockSpec((size, tile), lambda step, core: (0, step)) for size in sizes],
        ),
        out_shape=[jax.ShapeDtypeStruct((size, columns), BF16) for size in sizes],
        compiler_params=limit(28),
    )(core, in_hbm(own_weight), in_hbm(other_weight), *blocks, *half_blocks)


def choose_kernel(wanted, *refs, sources):
    for place, out in enumerate(refs[sources:]):
        for index, source in enumerate(refs[:sources]):
            @pl.when(wanted[place] == index)
            def _(out=out, source=source):
                out[...] = source[...]


def choose(wanted, sources, count):
    rows, columns = sources[0].shape
    spec = pl.BlockSpec((rows // CHOOSE_STEPS, columns), lambda step, wanted: (step, 0))
    return pl.pallas_call(
        functools.partial(choose_kernel, sources=len(sources)),
        grid_spec=pltpu.PrefetchScalarGridSpec(
            num_scalar_prefetch=1,
            grid=(CHOOSE_STEPS,),
            in_specs=[spec] * len(sources),
            out_specs=[spec] * count,
        ),
        out_shape=[jax.ShapeDtypeStruct((rows, columns), sources[0].dtype)] * count,
        compiler_params=limit(20),
    )(wanted, *sources)


def weight_kernel(core, *refs, blocks, grads, scale):
    rows = refs[:blocks]
    columns_of = refs[blocks:blocks + grads]
    kind_rows = refs[blocks + grads:blocks + 2 * grads]
    out, turned = refs[blocks + 2 * grads:]
    kinds, half, _ = out.shape

    @pl.when(pl.program_id(0) == 0)
    def _():
        kind = kinds_in([ref[...] for ref in kind_rows])
        start = 0
        for ref in rows:
            count = ref.shape[0]
            part = ref[:, pl.ds(pl.multiple_of(core[0] * half, half), half)].T
            own_kind = kind[:, start:start + count]
            for which in range(kinds):
                turned[which, :, start:start + count] = jnp.where(own_kind == which, part, 0)
            start += count

    columns = jnp.concatenate([ref[...] for ref in columns_of], axis=0)
    for which in range(kinds):
        total = jnp.dot(turned[which], columns, preferred_element_type=F32)
        out[which] = (total * scale).astype(BF16)


def weight_gradient(core, blocks, half_blocks, kinds, scale):
    rows, features = blocks[0].shape
    half = features // 2
    columns = half_blocks[0].shape[1]
    cut = half_blocks[0].shape[0] - KIND_ROWS
    tile = math.gcd(columns, WEIGHT_TILE)
    return pl.pallas_call(
        functools.partial(weight_kernel, blocks=len(blocks), grads=len(half_blocks), scale=scale),
        grid_spec=pltpu.PrefetchScalarGridSpec(
            num_scalar_prefetch=1,
            grid=(columns // tile,),
            in_specs=[whole(block.shape) for block in blocks]
            + [pl.BlockSpec((cut, tile), lambda step, core: (0, step)) for _ in half_blocks]
            + [kind_spec(block) for block in half_blocks],
            out_specs=pl.BlockSpec((kinds, half, tile), lambda step, core: (0, 0, step)),
            scratch_shapes=[pltpu.VMEM((kinds, half, rows * len(blocks)), BF16)],
        ),
        out_shape=jax.ShapeDtypeStruct((kinds, half, columns), BF16),
        compiler_params=limit(36),
    )(core, *blocks, *half_blocks, *half_blocks)


def low_high(offset):
    return offset & -offset, 1 << (offset.bit_length() - 1)


def body(tokens, out_grad, qkv_weight, dest_row, loop_modality):
    loop_count = lax.axis_size("loop")
    tp_count = lax.axis_size("tp")
    row_count, feature_part = tokens.shape
    kinds, half, _ = qkv_weight.shape
    chip_count = loop_count // 2
    assert chip_count == tp_count and 2 * half == feature_part
    capacity = 3 * row_count // (2 * loop_count)
    grad_scale = 1.0 / math.sqrt(row_count * loop_count)
    loop_index = lax.axis_index("loop")
    chip, level = loop_index >> 1, lax.axis_index("tp")
    core = (loop_index & 1).reshape(1)
    bits = [1 << place for place in range(chip_count.bit_length() - 1)]
    offsets = sorted(range(1, chip_count), key=lambda offset: (bin(offset).count("1"), offset))
    several = [offset for offset in offsets if offset & (offset - 1)]
    cut = row_count // 2

    def across(value, offset):
        pairs = [(i, i ^ (2 * offset)) for i in range(loop_count)]
        return lax.ppermute(value, "loop", pairs)

    def sibling(value):
        return lax.ppermute(value, "loop", [(i, i ^ 1) for i in range(loop_count)])

    def line_pairs(parity, stage):
        pairs = []
        for low in range(parity, tp_count - 1, 2):
            if low - stage + 1 >= 0:
                pairs.append((low, low + 1))
            if low + stage <= tp_count - 1:
                pairs.append((low + 1, low))
        return pairs

    def along(value, pairs):
        return lax.ppermute(value, "tp", pairs)

    stages = range(1, tp_count)
    facing = [jnp.where(level % 2 == parity, 1, -1) for parity in (0, 1)]

    other_weight = sibling(qkv_weight)
    came = {(0, 0): tokens, (1, 0): tokens}
    for stage in stages:
        for parity in (0, 1):
            pairs = line_pairs(parity, stage)
            if pairs:
                came[parity, stage] = along(came[1 - parity, stage - 1], pairs)

    own_grad = packed_grads(out_grad, dest_row, loop_modality, capacity)
    grads = {0: own_grad}
    for bit in bits:
        grads[bit] = [None, None]
    for bit in bits:
        first = 0 if bit == bits[-1] else 1
        for part in (first, 1 - first):
            grads[bit][part] = across(own_grad[part], bit)
    for offset in several:
        low, high = low_high(offset)
        grads[offset] = [across(grads[offset ^ low][0], low), across(grads[offset ^ high][1], high)]

    def halves_of(group):
        return [part for offset in group for part in grads[offset]]

    arrived = {}
    for group in ([0], bits, several):
        made = input_terms(
            core, halves_of(group), [row_count] * len(group), qkv_weight, other_weight
        )
        for offset, term in zip(group, made):
            arrived[offset] = across(term, offset) if offset else term
    all_terms = [arrived[offset] for offset in range(chip_count)]

    def level_term(where):
        offset = chip ^ jnp.clip(where, 0, tp_count - 1)
        term = all_terms[0]
        for index in range(1, chip_count):
            term = jnp.where(offset == index, all_terms[index], term)
        return term.astype(F32)

    back = {}
    for stage in reversed(stages):
        for parity in (0, 1):
            pairs = line_pairs(parity, stage)
            if pairs:
                value = level_term(level + stage * facing[parity])
                if (1 - parity, stage + 1) in back:
                    value = value + back[1 - parity, stage + 1].astype(F32)
                back[parity, stage] = along(value.astype(BF16), [(b, a) for a, b in pairs])
    input_grad = level_term(level)
    for parity in (0, 1):
        if (parity, 1) in back:
            input_grad = input_grad + back[parity, 1].astype(F32)
    input_grad = input_grad.astype(BF16)

    places = [place for place in came if place != (1, 0)]
    sources = [came[place] for place in places]
    wanted = []
    for offset in range(chip_count):
        where = chip ^ offset
        index = jnp.int32(0)
        for number, (parity, stage) in enumerate(places):
            if stage:
                index = jnp.where(where == level + stage * facing[parity], number, index)
        wanted.append(index)
    sends = choose(jnp.stack(wanted), sources, chip_count)
    rows = {
        offset: across(sends[offset], offset) if offset else sends[offset]
        for offset in range(chip_count)
    }

    parts = {}
    for group in (several, bits, [0]):
        made = project_parts(
            core, [rows[offset] for offset in group], halves_of(group),
            [cut] * (2 * len(group)), qkv_weight, other_weight,
        )
        for place, offset in enumerate(group):
            parts[offset] = [part.astype(F32) for part in made[2 * place:2 * place + 2]]
    for offset in reversed(several):
        low, high = low_high(offset)
        for part, (near, link) in enumerate(((offset ^ low, low), (offset ^ high, high))):
            piece = across(parts[offset][part].astype(BF16), link)
            parts[near][part] = parts[near][part] + piece.astype(F32)
    for bit in bits:
        for part in (0, 1):
            piece = across(parts[bit][part].astype(BF16), bit)
            parts[0][part] = parts[0][part] + piece.astype(F32)
    projected = jnp.concatenate([part.astype(BF16) for part in parts[0]], axis=0)

    near = [rows[offset] for offset in range(chip_count)]
    far = [sibling(block) for block in near]
    near_grads = halves_of(range(chip_count))
    far_grads = [sibling(block) for block in near_grads]
    weight_grad = weight_gradient(core, near + far, near_grads + far_grads, kinds, grad_scale)
    return projected, input_grad, weight_grad


def solution(mesh):
    placed = (P("loop", "tp"), P("loop", "tp"), P(None, "loop", "tp"), P("loop"), P())
    return jax.shard_map(
        body,
        mesh=mesh,
        in_specs=placed,
        out_specs=(P("loop", "tp"), P("loop", "tp"), P(None, "loop", "tp")),
        check_vma=False,
    )
```

```python
import functools
import math

import jax
import jax.numpy as jnp
from jax import lax
from jax.experimental import pallas as pl
from jax.experimental.pallas import tpu as pltpu
from jax.sharding import PartitionSpec as P


BF16 = jnp.bfloat16
F32 = jnp.float32
KIND_ROWS = 8
PROJECT_TILE = 512
CHOOSE_STEPS = 2
WEIGHT_TILE = 512


def pack_kernel(kinds_of_loops, dest, grads, *outs, capacity):
    slots = dest[...]
    found = jnp.full(slots.shape, kinds_of_loops[0], jnp.int32)
    for loop_index in range(1, kinds_of_loops.shape[0]):
        found = jnp.where(slots >= loop_index * capacity, kinds_of_loops[loop_index], found)
    cut = slots.shape[1] // len(outs)
    for part, out in enumerate(outs):
        extra = out.shape[0] - cut
        kind = found[:, part * cut:(part + 1) * cut].astype(F32).astype(BF16)
        out[:cut] = grads[part * cut:(part + 1) * cut]
        out[cut:] = jnp.zeros((extra, out.shape[1]), BF16)
        out[cut:, :cut] = jnp.broadcast_to(kind, (extra, cut))


def packed_grads(out_grad, dest_row, loop_modality, capacity):
    rows, columns = out_grad.shape
    slots = dest_row.reshape(1, -1)
    packed = (rows // 2 + KIND_ROWS, columns)
    return pl.pallas_call(
        functools.partial(pack_kernel, capacity=capacity),
        grid_spec=pltpu.PrefetchScalarGridSpec(
            num_scalar_prefetch=1,
            grid=(1,),
            in_specs=[whole(slots.shape), whole(out_grad.shape)],
            out_specs=[whole(packed), whole(packed)],
        ),
        out_shape=[jax.ShapeDtypeStruct(packed, BF16)] * 2,
        compiler_params=limit(8),
    )(loop_modality, *in_hbm(slots, out_grad))


def in_hbm(*values):
    return [pltpu.with_memory_space_constraint(value, pltpu.HBM) for value in values]


def kinds_in(refs):
    return jnp.concatenate([ref[:1].astype(F32) for ref in refs], axis=1)


def kind_spec(half_block):
    cut = half_block.shape[0] - KIND_ROWS
    return pl.BlockSpec((KIND_ROWS, cut), lambda *_: (cut // KIND_ROWS, 0))


def pick(kind, products):
    chosen = products[0]
    for index in range(1, len(products)):
        chosen = jnp.where(kind == index, products[index], chosen)
    return chosen


def whole(shape):
    return pl.BlockSpec(shape, lambda *_: (0,) * len(shape))


def split_rows(value, outs):
    start = 0
    for out in outs:
        yield out, value[start:start + out.shape[0]]
        start += out.shape[0]


def limit(mebibytes):
    return pltpu.CompilerParams(vmem_limit_bytes=mebibytes << 20)


def input_kernel(core, own_weight, other_weight, *refs, blocks, tile):
    cut = refs[0].shape[0] - KIND_ROWS
    rhs = jnp.concatenate([ref[:cut] for ref in refs[:blocks]], axis=0)
    kind = kinds_in([ref[cut:, :cut] for ref in refs[:blocks]])
    outs = refs[blocks:]
    half = outs[0].shape[1] // 2
    kinds, _, columns = own_weight.shape
    for weight, side in ((own_weight, core[0]), (other_weight, 1 - core[0])):
        product = lax.dot_general(
            weight[...].reshape(kinds * tile, columns), rhs, (((1,), (1,)), ((), ())),
            preferred_element_type=F32,
        )
        products = [product[index * tile:(index + 1) * tile] for index in range(kinds)]
        chosen = pick(kind, products).astype(BF16).T
        at = pl.multiple_of(side * half + pl.program_id(0) * tile, tile)
        for out, part in split_rows(chosen, outs):
            out[:, pl.ds(at, tile)] = part


def input_terms(core, blocks, sizes, own_weight, other_weight):
    kinds, half, columns = own_weight.shape
    tile = min(half, 256)
    weight_spec = pl.BlockSpec((kinds, tile, columns), lambda step, core: (0, step, 0))
    return pl.pallas_call(
        functools.partial(input_kernel, blocks=len(blocks), tile=tile),
        grid_spec=pltpu.PrefetchScalarGridSpec(
            num_scalar_prefetch=1,
            grid=(half // tile,),
            in_specs=[weight_spec, weight_spec] + [whole(block.shape) for block in blocks],
            out_specs=[whole((size, 2 * half)) for size in sizes],
        ),
        out_shape=[jax.ShapeDtypeStruct((size, 2 * half), BF16) for size in sizes],
        compiler_params=limit(28),
    )(core, *in_hbm(own_weight, other_weight, *blocks))


def project_kernel(core, own_weight, other_weight, *refs, counts):
    _, half, tile = own_weight.shape
    items = len(counts)
    own_at = pl.multiple_of(core[0] * half, half)
    other_at = pl.multiple_of((1 - core[0]) * half, half)
    own = jnp.concatenate([ref[:, pl.ds(own_at, half)] for ref in refs[:items]], axis=0)
    other = jnp.concatenate([ref[:, pl.ds(other_at, half)] for ref in refs[:items]], axis=0)
    kind = kinds_in([ref[...] for ref in refs[items:2 * items]])
    row_kind = jnp.broadcast_to(kind, (tile, kind.shape[1])).T
    products = [
        jnp.dot(own, own_weight[index], preferred_element_type=F32)
        + jnp.dot(other, other_weight[index], preferred_element_type=F32)
        for index in range(own_weight.shape[0])
    ]
    pieces = iter(refs[2 * items:2 * items + sum(counts)])
    outs = refs[2 * items + sum(counts):]
    for count, (out, part) in zip(counts, split_rows(pick(row_kind, products), outs)):
        for _ in range(count):
            part = part + next(pieces)[...].astype(F32)
        out[...] = part.astype(BF16)


def project_parts(core, items, own_weight, other_weight):
    kinds, half, columns = own_weight.shape
    tile = math.gcd(columns, PROJECT_TILE)
    weight_spec = pl.BlockSpec((kinds, half, tile), lambda step, core: (0, 0, step))
    cut = items[0][2].shape[0] - KIND_ROWS
    column_spec = pl.BlockSpec((cut, tile), lambda step, core: (0, step))
    row_specs = [pl.BlockSpec((cut, 2 * half), lambda step, core, part=part: (part, 0)) for _, part, _, _ in items]
    pieces = [piece for item in items for piece in item[3]]
    return pl.pallas_call(
        functools.partial(project_kernel, counts=[len(item[3]) for item in items]),
        grid_spec=pltpu.PrefetchScalarGridSpec(
            num_scalar_prefetch=1,
            grid=(columns // tile,),
            in_specs=[weight_spec, weight_spec]
            + row_specs
            + [kind_spec(item[2]) for item in items]
            + [column_spec] * len(pieces),
            out_specs=[column_spec] * len(items),
        ),
        out_shape=[jax.ShapeDtypeStruct((cut, columns), BF16)] * len(items),
        compiler_params=limit(28),
    )(core, *in_hbm(own_weight, other_weight, *[item[0] for item in items], *[item[2] for item in items], *pieces))


def finish_kernel(*refs, count):
    out = refs[-1]
    cut = out.shape[0] // 2
    for part in (0, 1):
        total = refs[part * count][...].astype(F32)
        for ref in refs[part * count + 1:(part + 1) * count]:
            total = total + ref[...].astype(F32)
        out[part * cut:(part + 1) * cut] = total.astype(BF16)


def finish(first, second):
    cut, columns = first[0].shape
    tile = math.gcd(columns, PROJECT_TILE)
    column_spec = pl.BlockSpec((cut, tile), lambda step: (0, step))
    return pl.pallas_call(
        functools.partial(finish_kernel, count=len(first)),
        grid=(columns // tile,),
        in_specs=[column_spec] * (2 * len(first)),
        out_specs=pl.BlockSpec((2 * cut, tile), lambda step: (0, step)),
        out_shape=jax.ShapeDtypeStruct((2 * cut, columns), BF16),
        compiler_params=limit(12),
    )(*in_hbm(*first, *second))


def choose_kernel(wanted, *refs, sources):
    for place, out in enumerate(refs[sources:]):
        for index, source in enumerate(refs[:sources]):
            @pl.when(wanted[place] == index)
            def _(out=out, source=source):
                out[...] = source[...]


def choose(wanted, sources, count):
    rows, columns = sources[0].shape
    spec = pl.BlockSpec((rows // CHOOSE_STEPS, columns), lambda step, wanted: (step, 0))
    return pl.pallas_call(
        functools.partial(choose_kernel, sources=len(sources)),
        grid_spec=pltpu.PrefetchScalarGridSpec(
            num_scalar_prefetch=1,
            grid=(CHOOSE_STEPS,),
            in_specs=[spec] * len(sources),
            out_specs=[spec] * count,
        ),
        out_shape=[jax.ShapeDtypeStruct((rows, columns), sources[0].dtype)] * count,
        compiler_params=limit(20),
    )(wanted, *in_hbm(*sources))


def weight_kernel(core, *refs, blocks, grads, scale):
    rows = refs[:blocks]
    columns_of = refs[blocks:blocks + grads]
    kind_rows = refs[blocks + grads:blocks + 2 * grads]
    out, turned = refs[blocks + 2 * grads:]
    kinds, half, _ = out.shape

    @pl.when(pl.program_id(0) == 0)
    def _():
        kind = kinds_in([ref[...] for ref in kind_rows])
        start = 0
        for ref in rows:
            count = ref.shape[0]
            part = ref[:, pl.ds(pl.multiple_of(core[0] * half, half), half)].T
            own_kind = kind[:, start:start + count]
            for which in range(kinds):
                turned[which, :, start:start + count] = jnp.where(own_kind == which, part, 0)
            start += count

    columns = jnp.concatenate([ref[...] for ref in columns_of], axis=0)
    for which in range(kinds):
        total = jnp.dot(turned[which], columns, preferred_element_type=F32)
        out[which] = (total * scale).astype(BF16)


def weight_gradient(core, blocks, half_blocks, kinds, scale):
    rows, features = blocks[0].shape
    half = features // 2
    columns = half_blocks[0].shape[1]
    cut = half_blocks[0].shape[0] - KIND_ROWS
    tile = math.gcd(columns, WEIGHT_TILE)
    return pl.pallas_call(
        functools.partial(weight_kernel, blocks=len(blocks), grads=len(half_blocks), scale=scale),
        grid_spec=pltpu.PrefetchScalarGridSpec(
            num_scalar_prefetch=1,
            grid=(columns // tile,),
            in_specs=[whole(block.shape) for block in blocks]
            + [pl.BlockSpec((cut, tile), lambda step, core: (0, step)) for _ in half_blocks]
            + [kind_spec(block) for block in half_blocks],
            out_specs=pl.BlockSpec((kinds, half, tile), lambda step, core: (0, 0, step)),
            scratch_shapes=[pltpu.VMEM((kinds, half, rows * len(blocks)), BF16)],
        ),
        out_shape=jax.ShapeDtypeStruct((kinds, half, columns), BF16),
        compiler_params=limit(36),
    )(core, *in_hbm(*blocks, *half_blocks, *half_blocks))


def low_high(offset):
    return offset & -offset, 1 << (offset.bit_length() - 1)


def body(tokens, out_grad, qkv_weight, dest_row, loop_modality):
    loop_count = lax.axis_size("loop")
    tp_count = lax.axis_size("tp")
    row_count, feature_part = tokens.shape
    kinds, half, _ = qkv_weight.shape
    chip_count = loop_count // 2
    assert chip_count == tp_count and 2 * half == feature_part
    capacity = 3 * row_count // (2 * loop_count)
    grad_scale = 1.0 / math.sqrt(row_count * loop_count)
    loop_index = lax.axis_index("loop")
    chip, level = loop_index >> 1, lax.axis_index("tp")
    core = (loop_index & 1).reshape(1)
    bits = [1 << place for place in range(chip_count.bit_length() - 1)]
    offsets = sorted(range(1, chip_count), key=lambda offset: (bin(offset).count("1"), offset))
    several = [offset for offset in offsets if offset & (offset - 1)]

    def across(value, offset):
        pairs = [(i, i ^ (2 * offset)) for i in range(loop_count)]
        return lax.ppermute(value, "loop", pairs)

    def sibling(value):
        return lax.ppermute(value, "loop", [(i, i ^ 1) for i in range(loop_count)])

    def line_pairs(parity, stage):
        pairs = []
        for low in range(parity, tp_count - 1, 2):
            if low - stage + 1 >= 0:
                pairs.append((low, low + 1))
            if low + stage <= tp_count - 1:
                pairs.append((low + 1, low))
        return pairs

    def along(value, pairs):
        return lax.ppermute(value, "tp", pairs)

    stages = range(1, tp_count)
    facing = [jnp.where(level % 2 == parity, 1, -1) for parity in (0, 1)]

    other_weight = sibling(qkv_weight)
    came = {(0, 0): tokens, (1, 0): tokens}
    for stage in stages:
        for parity in (0, 1):
            pairs = line_pairs(parity, stage)
            if pairs:
                came[parity, stage] = along(came[1 - parity, stage - 1], pairs)

    own_grad = packed_grads(out_grad, dest_row, loop_modality, capacity)
    grads = {0: own_grad}
    for bit in bits:
        grads[bit] = [None, None]
    for bit in bits:
        first = 0 if bit == bits[-1] else 1
        for part in (first, 1 - first):
            grads[bit][part] = across(own_grad[part], bit)
    for offset in several:
        low, high = low_high(offset)
        grads[offset] = [across(grads[offset ^ low][0], low), across(grads[offset ^ high][1], high)]

    def halves_of(group):
        return [part for offset in group for part in grads[offset]]

    arrived = {}
    for group in ([0], bits, several):
        made = input_terms(core, halves_of(group), [row_count] * len(group), qkv_weight, other_weight)
        for offset, term in zip(group, made):
            arrived[offset] = across(term, offset) if offset else term
    all_terms = [arrived[offset] for offset in range(chip_count)]

    def level_term(where):
        offset = chip ^ jnp.clip(where, 0, tp_count - 1)
        term = all_terms[0]
        for index in range(1, chip_count):
            term = jnp.where(offset == index, all_terms[index], term)
        return term.astype(F32)

    back = {}
    for stage in reversed(stages):
        for parity in (0, 1):
            pairs = line_pairs(parity, stage)
            if pairs:
                value = level_term(level + stage * facing[parity])
                if (1 - parity, stage + 1) in back:
                    value = value + back[1 - parity, stage + 1].astype(F32)
                back[parity, stage] = along(value.astype(BF16), [(b, a) for a, b in pairs])
    input_grad = level_term(level)
    for parity in (0, 1):
        if (parity, 1) in back:
            input_grad = input_grad + back[parity, 1].astype(F32)
    input_grad = input_grad.astype(BF16)

    places = [place for place in came if place != (1, 0)]
    sources = [came[place] for place in places]
    wanted = []
    for offset in range(chip_count):
        where = chip ^ offset
        index = jnp.int32(0)
        for number, (parity, stage) in enumerate(places):
            if stage:
                index = jnp.where(where == level + stage * facing[parity], number, index)
        wanted.append(index)
    sends = choose(jnp.stack(wanted), sources, chip_count)
    rows = {offset: across(sends[offset], offset) if offset else sends[offset] for offset in range(chip_count)}

    pieces = {(offset, part): [] for offset in range(chip_count) for part in (0, 1)}

    def project(places):
        items = [(rows[offset], part, grads[offset][part], pieces[offset, part] if offset else []) for offset, part in places]
        made = project_parts(core, items, qkv_weight, other_weight)
        return dict(zip(places, made))

    own_parts = project([(0, 0), (0, 1)])
    for weight in range(len(bits), 0, -1):
        places = [(offset, part) for offset in offsets if bin(offset).count("1") == weight for part in (0, 1)]
        bare = [place for place in places if not pieces[place]]
        summed = [place for place in places if pieces[place]]
        for some in (bare, summed):
            made = project(some) if some else {}
            for (offset, part), value in made.items():
                link = low_high(offset)[part]
                if offset in bits:
                    link = offset
                pieces[offset ^ link, part].append(across(value, link))
    projected = finish([own_parts[0, 0], *pieces[0, 0]], [own_parts[0, 1], *pieces[0, 1]])

    near = [rows[offset] for offset in range(chip_count)]
    far = [sibling(block) for block in near]
    near_grads = halves_of(range(chip_count))
    far_grads = [sibling(block) for block in near_grads]
    weight_grad = weight_gradient(core, near + far, near_grads + far_grads, kinds, grad_scale)
    return projected, input_grad, weight_grad


def solution(mesh):
    placed = (P("loop", "tp"), P("loop", "tp"), P(None, "loop", "tp"), P("loop"), P())
    return jax.shard_map(
        body,
        mesh=mesh,
        in_specs=placed,
        out_specs=(P("loop", "tp"), P("loop", "tp"), P(None, "loop", "tp")),
        check_vma=False,
    )
```

```python
import functools
import math

import jax
import jax.numpy as jnp
from jax import lax
from jax.experimental import pallas as pl
from jax.experimental.pallas import tpu as pltpu
from jax.sharding import PartitionSpec as P


BF16 = jnp.bfloat16
F32 = jnp.float32
KIND_ROWS = 8
PROJECT_TILE = 512
WEIGHT_TILE = 512


def pack_kernel(kinds_of_loops, dest, grads, *outs, capacity):
    slots = dest[...]
    found = jnp.full(slots.shape, kinds_of_loops[0], jnp.int32)
    for loop_index in range(1, kinds_of_loops.shape[0]):
        found = jnp.where(slots >= loop_index * capacity, kinds_of_loops[loop_index], found)
    cut = slots.shape[1] // len(outs)
    for part, out in enumerate(outs):
        extra = out.shape[0] - cut
        kind = found[:, part * cut:(part + 1) * cut].astype(F32).astype(BF16)
        out[:cut] = grads[part * cut:(part + 1) * cut]
        out[cut:] = jnp.zeros((extra, out.shape[1]), BF16)
        out[cut:, :cut] = jnp.broadcast_to(kind, (extra, cut))


def packed_grads(out_grad, dest_row, loop_modality, capacity):
    rows, columns = out_grad.shape
    slots = dest_row.reshape(1, -1)
    packed = (rows // 2 + KIND_ROWS, columns)
    return pl.pallas_call(
        functools.partial(pack_kernel, capacity=capacity),
        grid_spec=pltpu.PrefetchScalarGridSpec(
            num_scalar_prefetch=1,
            grid=(1,),
            in_specs=[whole(slots.shape), whole(out_grad.shape)],
            out_specs=[whole(packed), whole(packed)],
        ),
        out_shape=[pltpu.HBM(packed, BF16)] * 2,
        compiler_params=limit(8),
    )(loop_modality, *in_hbm(slots, out_grad))


def in_hbm(*values):
    return [pltpu.with_memory_space_constraint(value, pltpu.HBM) for value in values]


def kinds_in(refs):
    return jnp.concatenate([ref[:1].astype(F32) for ref in refs], axis=1)


def kind_spec(half_block):
    cut = half_block.shape[0] - KIND_ROWS
    return pl.BlockSpec((KIND_ROWS, cut), lambda *_: (cut // KIND_ROWS, 0))


def pick(kind, products):
    chosen = products[0]
    for index in range(1, len(products)):
        chosen = jnp.where(kind == index, products[index], chosen)
    return chosen


def whole(shape):
    return pl.BlockSpec(shape, lambda *_: (0,) * len(shape))


def split_rows(value, outs):
    start = 0
    for out in outs:
        yield out, value[start:start + out.shape[0]]
        start += out.shape[0]


def limit(mebibytes):
    return pltpu.CompilerParams(vmem_limit_bytes=mebibytes << 20)


def input_kernel(core, own_weight, other_weight, *refs, blocks, tile):
    cut = refs[0].shape[0] - KIND_ROWS
    rhs = jnp.concatenate([ref[:cut] for ref in refs[:blocks]], axis=0)
    kind = kinds_in([ref[cut:, :cut] for ref in refs[:blocks]])
    outs = refs[blocks:]
    half = outs[0].shape[1] // 2
    kinds, _, columns = own_weight.shape
    for weight, side in ((own_weight, core[0]), (other_weight, 1 - core[0])):
        product = lax.dot_general(
            weight[...].reshape(kinds * tile, columns), rhs, (((1,), (1,)), ((), ())),
            preferred_element_type=F32,
        )
        products = [product[index * tile:(index + 1) * tile] for index in range(kinds)]
        chosen = pick(kind, products).astype(BF16).T
        at = pl.multiple_of(side * half + pl.program_id(0) * tile, tile)
        for out, part in split_rows(chosen, outs):
            out[:, pl.ds(at, tile)] = part


def input_terms(core, blocks, sizes, own_weight, other_weight):
    kinds, half, columns = own_weight.shape
    tile = min(half, 256)
    weight_spec = pl.BlockSpec((kinds, tile, columns), lambda step, core: (0, step, 0))
    return pl.pallas_call(
        functools.partial(input_kernel, blocks=len(blocks), tile=tile),
        grid_spec=pltpu.PrefetchScalarGridSpec(
            num_scalar_prefetch=1,
            grid=(half // tile,),
            in_specs=[weight_spec, weight_spec] + [whole(block.shape) for block in blocks],
            out_specs=[whole((size, 2 * half)) for size in sizes],
        ),
        out_shape=[pltpu.HBM((size, 2 * half), BF16) for size in sizes],
        compiler_params=limit(28),
    )(core, *in_hbm(own_weight, other_weight, *blocks))


def project_kernel(core, own_weight, other_weight, *refs, items):
    _, half, tile = own_weight.shape
    own_at = pl.multiple_of(core[0] * half, half)
    other_at = pl.multiple_of((1 - core[0]) * half, half)
    own = jnp.concatenate([ref[:, pl.ds(own_at, half)] for ref in refs[:items]], axis=0)
    other = jnp.concatenate([ref[:, pl.ds(other_at, half)] for ref in refs[:items]], axis=0)
    kind = kinds_in([ref[...] for ref in refs[items:2 * items]])
    row_kind = jnp.broadcast_to(kind, (tile, kind.shape[1])).T
    products = [
        jnp.dot(own, own_weight[index], preferred_element_type=F32)
        + jnp.dot(other, other_weight[index], preferred_element_type=F32)
        for index in range(own_weight.shape[0])
    ]
    chosen = pick(row_kind, products).astype(BF16)
    for out, part in split_rows(chosen, refs[2 * items:]):
        out[...] = part


def project_parts(core, items, own_weight, other_weight):
    kinds, half, columns = own_weight.shape
    tile = math.gcd(columns, PROJECT_TILE)
    weight_spec = pl.BlockSpec((kinds, half, tile), lambda step, core: (0, 0, step))
    cut = items[0][2].shape[0] - KIND_ROWS
    return pl.pallas_call(
        functools.partial(project_kernel, items=len(items)),
        grid_spec=pltpu.PrefetchScalarGridSpec(
            num_scalar_prefetch=1,
            grid=(columns // tile,),
            in_specs=[weight_spec, weight_spec]
            + [pl.BlockSpec((cut, 2 * half), lambda step, core, part=item[1]: (part, 0)) for item in items]
            + [kind_spec(item[2]) for item in items],
            out_specs=[pl.BlockSpec((cut, tile), lambda step, core: (0, step))] * len(items),
        ),
        out_shape=[pltpu.HBM((cut, columns), BF16)] * len(items),
        compiler_params=limit(28),
    )(core, *in_hbm(own_weight, other_weight, *[item[0] for item in items], *[item[2] for item in items]))


def total_kernel(*refs, counts):
    outs = refs[sum(counts):]
    start = 0
    for count, out in zip(counts, outs):
        total = refs[start][...].astype(F32)
        for ref in refs[start + 1:start + count]:
            total = total + ref[...].astype(F32)
        out[...] = total.astype(BF16)
        start += count


def totals(groups):
    values = [value for group in groups for value in group]
    return pl.pallas_call(
        functools.partial(total_kernel, counts=[len(group) for group in groups]),
        grid=(1,),
        in_specs=[whole(value.shape) for value in values],
        out_specs=[whole(group[0].shape) for group in groups],
        out_shape=[pltpu.HBM(group[0].shape, BF16) for group in groups],
        compiler_params=limit(16),
    )(*in_hbm(*values))


def finish_kernel(*refs, count):
    out = refs[-1]
    cut = out.shape[0] // 2
    for part in (0, 1):
        total = refs[part * count][...].astype(F32)
        for ref in refs[part * count + 1:(part + 1) * count]:
            total = total + ref[...].astype(F32)
        out[part * cut:(part + 1) * cut] = total.astype(BF16)


def finish(first, second):
    cut, columns = first[0].shape
    return pl.pallas_call(
        functools.partial(finish_kernel, count=len(first)),
        grid=(1,),
        in_specs=[whole((cut, columns))] * (2 * len(first)),
        out_specs=whole((2 * cut, columns)),
        out_shape=jax.ShapeDtypeStruct((2 * cut, columns), BF16),
        compiler_params=limit(16),
    )(*in_hbm(*first, *second))


def fold_kernel(wanted, *refs, sources, counts):
    places = len(counts)
    added = refs[sources:sources + sum(counts)]
    outs = refs[sources + sum(counts):-2]
    held, done = refs[-2:]
    for place in range(places):
        for index in range(sources):
            @pl.when(wanted[place] == index)
            def _(place=place, index=index):
                pltpu.make_async_copy(refs[index], held.at[place], done.at[place]).start()
    start = 0
    for place, (count, out) in enumerate(zip(counts, outs)):
        pltpu.make_async_copy(refs[0], held.at[place], done.at[place]).wait()
        if count:
            total = held[place].astype(F32)
            for ref in added[start:start + count]:
                total = total + ref[...].astype(F32)
            out[...] = total.astype(BF16)
        else:
            out[...] = held[place]
        start += count


def fold(wanted, sources, groups):
    shape = sources[0].shape
    values = [value for group in groups for value in group]
    return pl.pallas_call(
        functools.partial(fold_kernel, sources=len(sources), counts=[len(group) for group in groups]),
        grid_spec=pltpu.PrefetchScalarGridSpec(
            num_scalar_prefetch=1,
            grid=(1,),
            in_specs=[pl.BlockSpec(memory_space=pl.ANY)] * len(sources) + [whole(shape)] * len(values),
            out_specs=[whole(shape)] * len(groups),
            scratch_shapes=[
                pltpu.VMEM((len(groups), *shape), BF16), pltpu.SemaphoreType.DMA((len(groups),))
            ],
        ),
        out_shape=[pltpu.HBM(shape, BF16)] * len(groups),
        compiler_params=limit(20),
    )(jnp.stack(wanted), *sources, *values)


def weight_kernel(core, *refs, blocks, grads, scale):
    rows = refs[:blocks]
    columns_of = refs[blocks:blocks + grads]
    kind_rows = refs[blocks + grads:blocks + 2 * grads]
    out, turned = refs[blocks + 2 * grads:]
    kinds, _, _ = out.shape

    @pl.when(pl.program_id(0) == 0)
    def _():
        kind = kinds_in([ref[...] for ref in kind_rows])
        start = 0
        for ref in rows:
            count = ref.shape[0]
            part = ref[...].T
            own_kind = kind[:, start:start + count]
            for which in range(kinds):
                turned[which, :, start:start + count] = jnp.where(own_kind == which, part, 0)
            start += count

    columns = jnp.concatenate([ref[...] for ref in columns_of], axis=0)
    for which in range(kinds):
        total = jnp.dot(turned[which], columns, preferred_element_type=F32)
        out[which] = (total * scale).astype(BF16)


def weight_gradient(core, blocks, half_blocks, kinds, scale):
    rows, features = blocks[0].shape
    half = features // 2
    columns = half_blocks[0].shape[1]
    cut = half_blocks[0].shape[0] - KIND_ROWS
    tile = math.gcd(columns, WEIGHT_TILE)
    return pl.pallas_call(
        functools.partial(weight_kernel, blocks=len(blocks), grads=len(half_blocks), scale=scale),
        grid_spec=pltpu.PrefetchScalarGridSpec(
            num_scalar_prefetch=1,
            grid=(columns // tile,),
            in_specs=[pl.BlockSpec((rows, half), lambda step, core: (0, core[0])) for _ in blocks]
            + [pl.BlockSpec((cut, tile), lambda step, core: (0, step)) for _ in half_blocks]
            + [kind_spec(block) for block in half_blocks],
            out_specs=pl.BlockSpec((kinds, half, tile), lambda step, core: (0, 0, step)),
            scratch_shapes=[pltpu.VMEM((kinds, half, rows * len(blocks)), BF16)],
        ),
        out_shape=jax.ShapeDtypeStruct((kinds, half, columns), BF16),
        compiler_params=limit(36),
    )(core, *in_hbm(*blocks, *half_blocks, *half_blocks))


def low_high(offset):
    return offset & -offset, 1 << (offset.bit_length() - 1)


def body(tokens, out_grad, qkv_weight, dest_row, loop_modality):
    loop_count = lax.axis_size("loop")
    tp_count = lax.axis_size("tp")
    row_count, feature_part = tokens.shape
    kinds, half, _ = qkv_weight.shape
    chip_count = loop_count // 2
    assert chip_count == tp_count and 2 * half == feature_part
    capacity = 3 * row_count // (2 * loop_count)
    grad_scale = 1.0 / math.sqrt(row_count * loop_count)
    loop_index = lax.axis_index("loop")
    chip, level = loop_index >> 1, lax.axis_index("tp")
    core = (loop_index & 1).reshape(1)
    bits = [1 << place for place in range(chip_count.bit_length() - 1)]
    offsets = sorted(range(1, chip_count), key=lambda offset: (bin(offset).count("1"), offset))
    several = [offset for offset in offsets if offset & (offset - 1)]

    def across(value, offset):
        pairs = [(i, i ^ (2 * offset)) for i in range(loop_count)]
        return lax.ppermute(value, "loop", pairs)

    def sibling(value):
        return lax.ppermute(value, "loop", [(i, i ^ 1) for i in range(loop_count)])

    def line_pairs(parity, stage):
        pairs = []
        for low in range(parity, tp_count - 1, 2):
            if low - stage + 1 >= 0:
                pairs.append((low, low + 1))
            if low + stage <= tp_count - 1:
                pairs.append((low + 1, low))
        return pairs

    def along(value, pairs):
        return lax.ppermute(value, "tp", pairs)

    stages = range(1, tp_count)
    facing = [jnp.where(level % 2 == parity, 1, -1) for parity in (0, 1)]

    other_weight = sibling(qkv_weight)
    came = {(0, 0): tokens, (1, 0): tokens}
    for stage in stages:
        for parity in (0, 1):
            pairs = line_pairs(parity, stage)
            if pairs:
                came[parity, stage] = along(came[1 - parity, stage - 1], pairs)

    own_grad = packed_grads(out_grad, dest_row, loop_modality, capacity)
    grads = {0: own_grad}
    for bit in bits:
        grads[bit] = [None, None]
    for bit in bits:
        first = 0 if bit == bits[-1] else 1
        for part in (first, 1 - first):
            grads[bit][part] = across(own_grad[part], bit)
    for offset in several:
        low, high = low_high(offset)
        grads[offset] = [across(grads[offset ^ low][0], low), across(grads[offset ^ high][1], high)]

    def halves_of(group):
        return [part for offset in group for part in grads[offset]]

    arrived = {}
    for group in ([0], bits, several):
        made = input_terms(core, halves_of(group), [row_count] * len(group), qkv_weight, other_weight)
        for offset, term in zip(group, made):
            arrived[offset] = across(term, offset) if offset else term
    all_terms = [arrived[offset] for offset in range(chip_count)]

    def term_number(where):
        return chip ^ jnp.clip(where, 0, tp_count - 1)

    back = {}
    for stage in reversed(stages):
        links = [parity for parity in (0, 1) if line_pairs(parity, stage)]
        wanted = [term_number(level + stage * facing[parity]) for parity in links]
        groups = [[back[1 - parity, stage + 1]] if (1 - parity, stage + 1) in back else [] for parity in links]
        made = fold(wanted, all_terms, groups)
        for parity, value in zip(links, made):
            pairs = [(b, a) for a, b in line_pairs(parity, stage)]
            back[parity, stage] = along(value, pairs)
    last = [back[parity, 1] for parity in (0, 1) if (parity, 1) in back]
    input_grad = fold([term_number(level)], all_terms, [last])[0]

    places = [place for place in came if place != (1, 0)]
    sources = [came[place] for place in places]
    wanted = []
    for offset in range(chip_count):
        where = chip ^ offset
        index = jnp.int32(0)
        for number, (parity, stage) in enumerate(places):
            if stage:
                index = jnp.where(where == level + stage * facing[parity], number, index)
        wanted.append(index)
    sends = fold(wanted, in_hbm(*sources), [[]] * chip_count)
    rows = {offset: across(sends[offset], offset) if offset else sends[offset] for offset in range(chip_count)}

    pieces = {(offset, part): [] for offset in range(chip_count) for part in (0, 1)}

    def project(places):
        items = [(rows[offset], part, grads[offset][part]) for offset, part in places]
        made = project_parts(core, items, qkv_weight, other_weight)
        return dict(zip(places, made))

    own_parts = project([(0, 0), (0, 1)])
    for weight in range(len(bits), 0, -1):
        places = [(offset, part) for offset in offsets if bin(offset).count("1") == weight for part in (0, 1)]
        made = project(places)
        summed = [place for place in places if pieces[place]]
        if summed:
            sums = totals([[made[place], *pieces[place]] for place in summed])
            made.update(zip(summed, sums))
        for offset, part in places:
            link = offset if offset in bits else low_high(offset)[part]
            piece = across(made[offset, part], link)
            pieces[offset ^ link, part].append(piece)
    projected = finish([own_parts[0, 0], *pieces[0, 0]], [own_parts[0, 1], *pieces[0, 1]])

    near = [rows[offset] for offset in range(chip_count)]
    far = [sibling(block) for block in near]
    near_grads = halves_of(range(chip_count))
    far_grads = [sibling(block) for block in near_grads]
    weight_grad = weight_gradient(core, near + far, near_grads + far_grads, kinds, grad_scale)
    return projected, input_grad, weight_grad


def solution(mesh):
    placed = (P("loop", "tp"), P("loop", "tp"), P(None, "loop", "tp"), P("loop"), P())
    return jax.shard_map(
        body,
        mesh=mesh,
        in_specs=placed,
        out_specs=(P("loop", "tp"), P("loop", "tp"), P(None, "loop", "tp")),
        check_vma=False,
    )
```

```python
import functools
import math

import jax
import jax.numpy as jnp
from jax import lax
from jax.experimental import pallas as pl
from jax.experimental.pallas import tpu as pltpu
from jax.sharding import PartitionSpec as P


BF16 = jnp.bfloat16
F32 = jnp.float32
KIND_ROWS = 8
PART_KINDS = ((0, 1), (2, 1))
PROJECT_TILE = 512
WEIGHT_TILE = 512


def placing(place, dtype=BF16):
    count = place.shape[1]
    rows = lax.broadcasted_iota(jnp.int32, (count, count), 0)
    return (rows == place.astype(jnp.int32)).astype(F32).astype(dtype)


def pack_kernel(kinds_of_loops, dest, grads, first, second, places, *, capacity, kinds):
    slots = dest[...]
    found = jnp.full(slots.shape, kinds_of_loops[0], jnp.int32)
    for loop_index in range(1, kinds_of_loops.shape[0]):
        found = jnp.where(slots >= loop_index * capacity, kinds_of_loops[loop_index], found)
    count = slots.shape[1]
    upto = lax.broadcasted_iota(jnp.int32, (count, count), 0) <= lax.broadcasted_iota(jnp.int32, (count, count), 1)
    upto = upto.astype(F32).astype(BF16)
    lane = lax.broadcasted_iota(jnp.int32, (1, count), 1).astype(F32)
    place = jnp.zeros((1, count), F32)
    kind = jnp.zeros((1, count), F32)
    start = jnp.zeros((1, 1), F32)
    for which in range(kinds):
        mine = (found == which).astype(F32)
        counted = jnp.dot(
            jnp.broadcast_to(mine, (8, count)).astype(BF16), upto, preferred_element_type=F32
        )[:1]
        place = place + mine * (start + counted - 1.0)
        if which:
            kind = kind + (lane >= start).astype(F32)
        start = start + jnp.sum(mine, axis=1, keepdims=True)
    places[...] = jnp.broadcast_to(place, places.shape)
    ordered = jnp.dot(placing(place), grads[...], preferred_element_type=F32).astype(BF16)
    cut = count // 2
    for part, out in enumerate((first, second)):
        extra = out.shape[0] - cut
        out[:cut] = ordered[part * cut:(part + 1) * cut]
        out[cut:] = jnp.zeros((extra, out.shape[1]), BF16)
        out[cut:, :cut] = jnp.broadcast_to(kind[:, part * cut:(part + 1) * cut], (extra, cut)).astype(BF16)


def packed_grads(out_grad, dest_row, loop_modality, capacity, kinds):
    rows, columns = out_grad.shape
    slots = dest_row.reshape(1, -1)
    packed = (rows // 2 + KIND_ROWS, columns)
    return pl.pallas_call(
        functools.partial(pack_kernel, capacity=capacity, kinds=kinds),
        grid_spec=pltpu.PrefetchScalarGridSpec(
            num_scalar_prefetch=1,
            grid=(1,),
            in_specs=[whole(slots.shape), whole(out_grad.shape)],
            out_specs=[whole(packed), whole(packed), whole((8, rows))],
        ),
        out_shape=[
            jax.ShapeDtypeStruct(packed, BF16), jax.ShapeDtypeStruct(packed, BF16), pltpu.HBM((8, rows), F32)
        ],
        compiler_params=limit(60),
    )(loop_modality, *in_hbm(slots, out_grad))


def sort_kernel(places, rows, out):
    out[...] = jnp.dot(placing(places[:1]), rows[...], preferred_element_type=F32).astype(BF16)


def sorted_rows(places, rows):
    return pl.pallas_call(
        sort_kernel,
        grid=(1,),
        in_specs=[whole(places.shape), whole(rows.shape)],
        out_specs=whole(rows.shape),
        out_shape=pltpu.HBM(rows.shape, BF16),
        compiler_params=limit(16),
    )(*in_hbm(places, rows))


def in_hbm(*values):
    return [pltpu.with_memory_space_constraint(value, pltpu.HBM) for value in values]


def kinds_in(refs):
    return jnp.concatenate([ref[:1].astype(F32) for ref in refs], axis=1)


def kind_spec(half_block):
    cut = half_block.shape[0] - KIND_ROWS
    return pl.BlockSpec((KIND_ROWS, cut), lambda *_: (cut // KIND_ROWS, 0))


def whole(shape):
    return pl.BlockSpec(shape, lambda *_: (0,) * len(shape))


def limit(mebibytes):
    return pltpu.CompilerParams(vmem_limit_bytes=mebibytes << 20)


def input_kernel(core, own_weight, other_weight, *refs, blocks, tile):
    cut = refs[0].shape[0] - KIND_ROWS
    halves = [refs[part:blocks:2] for part in (0, 1)]
    sides = [jnp.concatenate([ref[:cut] for ref in some], axis=0) for some in halves]
    kinds = [kinds_in([ref[cut:, :cut] for ref in some]) for some in halves]
    outs = refs[blocks:]
    half = outs[0].shape[1] // 2

    def product(weight, rows):
        return lax.dot_general(weight, rows, (((1,), (1,)), ((), ())), preferred_element_type=F32)

    for weight, side in ((own_weight, core[0]), (other_weight, 1 - core[0])):
        common = product(weight[1], jnp.concatenate(sides, axis=0))
        at = pl.multiple_of(side * half + pl.program_id(0) * tile, tile)
        span = sides[0].shape[0]
        for part, (special, _) in enumerate(PART_KINDS):
            mine = product(weight[special], sides[part])
            chosen = jnp.where(kinds[part] == special, mine, common[:, part * span:(part + 1) * span])
            chosen = chosen.astype(BF16).T
            for number, out in enumerate(outs):
                out[part * cut:(part + 1) * cut, pl.ds(at, tile)] = chosen[number * cut:(number + 1) * cut]


def input_terms(core, blocks, sizes, own_weight, other_weight):
    kinds, half, columns = own_weight.shape
    tile = min(half, 256)
    weight_spec = pl.BlockSpec((kinds, tile, columns), lambda step, core: (0, step, 0))
    return pl.pallas_call(
        functools.partial(input_kernel, blocks=len(blocks), tile=tile),
        grid_spec=pltpu.PrefetchScalarGridSpec(
            num_scalar_prefetch=1,
            grid=(half // tile,),
            in_specs=[weight_spec, weight_spec] + [whole(block.shape) for block in blocks],
            out_specs=[whole((size, 2 * half)) for size in sizes],
        ),
        out_shape=[pltpu.HBM((size, 2 * half), BF16) for size in sizes],
        compiler_params=limit(28),
    )(core, *in_hbm(own_weight, other_weight, *blocks))


def project_kernel(core, own_weight, other_weight, *refs, items):
    _, half, tile = own_weight.shape
    own_at = pl.multiple_of(core[0] * half, half)
    other_at = pl.multiple_of((1 - core[0]) * half, half)
    own = jnp.concatenate([ref[:, pl.ds(own_at, half)] for ref in refs[:items]], axis=0)
    other = jnp.concatenate([ref[:, pl.ds(other_at, half)] for ref in refs[:items]], axis=0)
    kind = kinds_in([ref[...] for ref in refs[items:2 * items]])
    row_kind = jnp.broadcast_to(kind, (tile, kind.shape[1])).T
    outs = refs[2 * items:]

    def product(which, rows):
        return (
            jnp.dot(own[rows], own_weight[which], preferred_element_type=F32)
            + jnp.dot(other[rows], other_weight[which], preferred_element_type=F32)
        )

    span = own.shape[0] // 2
    cut = outs[0].shape[0]
    common = product(1, slice(None))
    for part, (special, _) in enumerate(PART_KINDS):
        rows = slice(part * span, (part + 1) * span)
        chosen = jnp.where(row_kind[rows] == special, product(special, rows), common[rows]).astype(BF16)
        for number in range(items // 2):
            outs[part * (items // 2) + number][...] = chosen[number * cut:(number + 1) * cut]


def project_parts(core, items, own_weight, other_weight):
    kinds, half, columns = own_weight.shape
    tile = math.gcd(columns, PROJECT_TILE)
    weight_spec = pl.BlockSpec((kinds, half, tile), lambda step, core: (0, 0, step))
    cut = items[0][2].shape[0] - KIND_ROWS
    return pl.pallas_call(
        functools.partial(project_kernel, items=len(items)),
        grid_spec=pltpu.PrefetchScalarGridSpec(
            num_scalar_prefetch=1,
            grid=(columns // tile,),
            in_specs=[weight_spec, weight_spec]
            + [pl.BlockSpec((cut, 2 * half), lambda step, core, part=item[1]: (part, 0)) for item in items]
            + [kind_spec(item[2]) for item in items],
            out_specs=[pl.BlockSpec((cut, tile), lambda step, core: (0, step))] * len(items),
        ),
        out_shape=[pltpu.HBM((cut, columns), BF16)] * len(items),
        compiler_params=limit(28),
    )(core, *in_hbm(own_weight, other_weight, *[item[0] for item in items], *[item[2] for item in items]))


def total_kernel(*refs, counts):
    outs = refs[sum(counts):]
    start = 0
    for count, out in zip(counts, outs):
        total = refs[start][...].astype(F32)
        for ref in refs[start + 1:start + count]:
            total = total + ref[...].astype(F32)
        out[...] = total.astype(BF16)
        start += count


def totals(groups):
    values = [value for group in groups for value in group]
    return pl.pallas_call(
        functools.partial(total_kernel, counts=[len(group) for group in groups]),
        grid=(1,),
        in_specs=[whole(value.shape) for value in values],
        out_specs=[whole(group[0].shape) for group in groups],
        out_shape=[pltpu.HBM(group[0].shape, BF16) for group in groups],
        compiler_params=limit(16),
    )(*in_hbm(*values))


def finish_kernel(places, term, *refs, count):
    projected, input_grad = refs[-2:]
    sums = []
    for part in (0, 1):
        total = refs[part * count][...].astype(F32)
        for ref in refs[part * count + 1:(part + 1) * count]:
            total = total + ref[...].astype(F32)
        sums.append(total.astype(BF16))
    back = placing(places[:1], F32).T.astype(BF16)
    projected[...] = jnp.dot(back, jnp.concatenate(sums, axis=0), preferred_element_type=F32).astype(BF16)
    input_grad[...] = jnp.dot(back, term[...], preferred_element_type=F32).astype(BF16)


def finish(places, term, first, second):
    cut, columns = first[0].shape
    shapes = ((2 * cut, columns), term.shape)
    return pl.pallas_call(
        functools.partial(finish_kernel, count=len(first)),
        grid=(1,),
        in_specs=[whole(places.shape), whole(term.shape)] + [whole((cut, columns))] * (2 * len(first)),
        out_specs=[whole(shape) for shape in shapes],
        out_shape=[jax.ShapeDtypeStruct(shape, BF16) for shape in shapes],
        compiler_params=limit(20),
    )(*in_hbm(places), term, *in_hbm(*first, *second))


def fold_kernel(wanted, *refs, sources, counts):
    places = len(counts)
    added = refs[sources:sources + sum(counts)]
    outs = refs[sources + sum(counts):-2]
    held, done = refs[-2:]
    for place in range(places):
        for index in range(sources):
            @pl.when(wanted[place] == index)
            def _(place=place, index=index):
                pltpu.make_async_copy(refs[index], held.at[place], done.at[place]).start()
    start = 0
    for place, (count, out) in enumerate(zip(counts, outs)):
        pltpu.make_async_copy(refs[0], held.at[place], done.at[place]).wait()
        if count:
            total = held[place].astype(F32)
            for ref in added[start:start + count]:
                total = total + ref[...].astype(F32)
            out[...] = total.astype(BF16)
        else:
            out[...] = held[place]
        start += count


def fold(wanted, sources, groups):
    shape = sources[0].shape
    values = [value for group in groups for value in group]
    return pl.pallas_call(
        functools.partial(fold_kernel, sources=len(sources), counts=[len(group) for group in groups]),
        grid_spec=pltpu.PrefetchScalarGridSpec(
            num_scalar_prefetch=1,
            grid=(1,),
            in_specs=[pl.BlockSpec(memory_space=pl.ANY)] * len(sources) + [whole(shape)] * len(values),
            out_specs=[whole(shape)] * len(groups),
            scratch_shapes=[
                pltpu.VMEM((len(groups), *shape), BF16), pltpu.SemaphoreType.DMA((len(groups),))
            ],
        ),
        out_shape=[pltpu.HBM(shape, BF16)] * len(groups),
        compiler_params=limit(20),
    )(jnp.stack(wanted), *sources, *values)


def weight_kernel(core, *refs, blocks, grads, scale):
    rows = refs[:blocks]
    columns_of = refs[blocks:blocks + grads]
    kind_rows = refs[blocks + grads:blocks + 2 * grads]
    out, *turned = refs[blocks + 2 * grads:]

    @pl.when(pl.program_id(0) == 0)
    def _():
        for number, ref in enumerate(rows):
            cut = ref.shape[0] // 2
            block = ref[...].T
            for part, part_kinds in enumerate(PART_KINDS):
                own_kind = kind_rows[2 * number + part][:1].astype(F32)
                for place, which in enumerate(part_kinds):
                    turned[part][place, :, number * cut:(number + 1) * cut] = jnp.where(
                        own_kind == which, block[:, part * cut:(part + 1) * cut], 0
                    )

    columns = [jnp.concatenate([ref[...] for ref in columns_of[part::2]], axis=0) for part in (0, 1)]
    common = sum(jnp.dot(turned[part][1], columns[part], preferred_element_type=F32) for part in (0, 1))
    out[1] = (common * scale).astype(BF16)
    for part, (special, _) in enumerate(PART_KINDS):
        total = jnp.dot(turned[part][0], columns[part], preferred_element_type=F32)
        out[special] = (total * scale).astype(BF16)


def weight_gradient(core, blocks, half_blocks, kinds, scale):
    rows, features = blocks[0].shape
    half = features // 2
    columns = half_blocks[0].shape[1]
    cut = half_blocks[0].shape[0] - KIND_ROWS
    tile = math.gcd(columns, WEIGHT_TILE)
    return pl.pallas_call(
        functools.partial(weight_kernel, blocks=len(blocks), grads=len(half_blocks), scale=scale),
        grid_spec=pltpu.PrefetchScalarGridSpec(
            num_scalar_prefetch=1,
            grid=(columns // tile,),
            in_specs=[pl.BlockSpec((rows, half), lambda step, core: (0, core[0])) for _ in blocks]
            + [pl.BlockSpec((cut, tile), lambda step, core: (0, step)) for _ in half_blocks]
            + [kind_spec(block) for block in half_blocks],
            out_specs=pl.BlockSpec((kinds, half, tile), lambda step, core: (0, 0, step)),
            scratch_shapes=[pltpu.VMEM((2, half, rows // 2 * len(blocks)), BF16)] * 2,
        ),
        out_shape=jax.ShapeDtypeStruct((kinds, half, columns), BF16),
        compiler_params=limit(36),
    )(core, *in_hbm(*blocks, *half_blocks, *half_blocks))


def low_high(offset):
    return offset & -offset, 1 << (offset.bit_length() - 1)


def body(tokens, out_grad, qkv_weight, dest_row, loop_modality):
    loop_count = lax.axis_size("loop")
    tp_count = lax.axis_size("tp")
    row_count, feature_part = tokens.shape
    kinds, half, _ = qkv_weight.shape
    chip_count = loop_count // 2
    assert chip_count == tp_count and 2 * half == feature_part
    capacity = 3 * row_count // (2 * loop_count)
    grad_scale = 1.0 / math.sqrt(row_count * loop_count)
    loop_index = lax.axis_index("loop")
    chip, level = loop_index >> 1, lax.axis_index("tp")
    core = (loop_index & 1).reshape(1)
    bits = [1 << place for place in range(chip_count.bit_length() - 1)]
    offsets = sorted(range(1, chip_count), key=lambda offset: (bin(offset).count("1"), offset))
    several = [offset for offset in offsets if offset & (offset - 1)]
    cut = row_count // 2

    def across(value, offset):
        pairs = [(i, i ^ (2 * offset)) for i in range(loop_count)]
        return lax.ppermute(value, "loop", pairs)

    def sibling(value):
        return lax.ppermute(value, "loop", [(i, i ^ 1) for i in range(loop_count)])

    def line_pairs(parity, stage):
        pairs = []
        for low in range(parity, tp_count - 1, 2):
            if low - stage + 1 >= 0:
                pairs.append((low, low + 1))
            if low + stage <= tp_count - 1:
                pairs.append((low + 1, low))
        return pairs

    def along(value, pairs):
        return lax.ppermute(value, "tp", pairs)

    stages = range(1, tp_count)
    facing = [jnp.where(level % 2 == parity, 1, -1) for parity in (0, 1)]

    assert kinds == 3 and capacity * loop_count // 4 <= cut
    other_weight = sibling(qkv_weight)
    *own_grad, order = packed_grads(out_grad, dest_row, loop_modality, capacity, kinds)
    tokens = sorted_rows(order, tokens)
    came = {(0, 0): tokens, (1, 0): tokens}
    for stage in stages:
        for parity in (0, 1):
            pairs = line_pairs(parity, stage)
            if pairs:
                came[parity, stage] = along(came[1 - parity, stage - 1], pairs)

    grads = {0: own_grad}
    for bit in bits:
        grads[bit] = [None, None]
    for bit in bits:
        first = 0 if bit == bits[-1] else 1
        for part in (first, 1 - first):
            grads[bit][part] = across(own_grad[part], bit)
    for offset in several:
        low, high = low_high(offset)
        grads[offset] = [across(grads[offset ^ low][0], low), across(grads[offset ^ high][1], high)]

    def halves_of(group):
        return [part for offset in group for part in grads[offset]]

    arrived = {}
    for group in ([0], bits, several):
        made = input_terms(core, halves_of(group), [row_count] * len(group), qkv_weight, other_weight)
        for offset, term in zip(group, made):
            arrived[offset] = across(term, offset) if offset else term
    all_terms = [arrived[offset] for offset in range(chip_count)]

    def term_number(where):
        return chip ^ jnp.clip(where, 0, tp_count - 1)

    back = {}
    for stage in reversed(stages):
        links = [parity for parity in (0, 1) if line_pairs(parity, stage)]
        wanted = [term_number(level + stage * facing[parity]) for parity in links]
        groups = [[back[1 - parity, stage + 1]] if (1 - parity, stage + 1) in back else [] for parity in links]
        made = fold(wanted, all_terms, groups)
        for parity, value in zip(links, made):
            pairs = [(b, a) for a, b in line_pairs(parity, stage)]
            back[parity, stage] = along(value, pairs)
    last = [back[parity, 1] for parity in (0, 1) if (parity, 1) in back]
    own_input = fold([term_number(level)], all_terms, [last])[0]

    places = [place for place in came if place != (1, 0)]
    sources = [came[place] for place in places]
    wanted = []
    for offset in range(chip_count):
        where = chip ^ offset
        index = jnp.int32(0)
        for number, (parity, stage) in enumerate(places):
            if stage:
                index = jnp.where(where == level + stage * facing[parity], number, index)
        wanted.append(index)
    sends = fold(wanted, in_hbm(*sources), [[]] * chip_count)
    rows = {offset: across(sends[offset], offset) if offset else sends[offset] for offset in range(chip_count)}

    pieces = {(offset, part): [] for offset in range(chip_count) for part in (0, 1)}

    def project(places):
        places = sorted(places, key=lambda place: place[1])
        items = [(rows[offset], part, grads[offset][part]) for offset, part in places]
        made = project_parts(core, items, qkv_weight, other_weight)
        return dict(zip(places, made))

    own_parts = project([(0, 0), (0, 1)])
    for weight in range(len(bits), 0, -1):
        places = [(offset, part) for offset in offsets if bin(offset).count("1") == weight for part in (0, 1)]
        made = project(places)
        summed = [place for place in places if pieces[place]]
        if summed:
            sums = totals([[made[place], *pieces[place]] for place in summed])
            made.update(zip(summed, sums))
        for offset, part in places:
            link = offset if offset in bits else low_high(offset)[part]
            piece = across(made[offset, part], link)
            pieces[offset ^ link, part].append(piece)
    projected, input_grad = finish(order, own_input, [own_parts[0, 0], *pieces[0, 0]], [own_parts[0, 1], *pieces[0, 1]])

    near = [rows[offset] for offset in range(chip_count)]
    far = [sibling(block) for block in near]
    near_grads = halves_of(range(chip_count))
    far_grads = [sibling(block) for block in near_grads]
    weight_grad = weight_gradient(core, near + far, near_grads + far_grads, kinds, grad_scale)
    return projected, input_grad, weight_grad


def solution(mesh):
    placed = (P("loop", "tp"), P("loop", "tp"), P(None, "loop", "tp"), P("loop"), P())
    return jax.shard_map(
        body,
        mesh=mesh,
        in_specs=placed,
        out_specs=(P("loop", "tp"), P("loop", "tp"), P(None, "loop", "tp")),
        check_vma=False,
    )
```

```python
import functools
import math

import jax
import jax.numpy as jnp
from jax import lax
from jax.experimental import pallas as pl
from jax.experimental.pallas import tpu as pltpu
from jax.sharding import PartitionSpec as P


BF16 = jnp.bfloat16
F32 = jnp.float32
KIND_ROWS = 8
PART_KINDS = ((0, 1), (2, 1))
PROJECT_TILE = 512
WEIGHT_TILE = 512


def placing(place, dtype=BF16):
    count = place.shape[1]
    rows = lax.broadcasted_iota(jnp.int32, (count, count), 0)
    return (rows == place.astype(jnp.int32)).astype(F32).astype(dtype)


def pack_kernel(kinds_of_loops, dest, grads, first, second, places, *, capacity, kinds):
    slots = dest[...]
    found = jnp.full(slots.shape, kinds_of_loops[0], jnp.int32)
    for loop_index in range(1, kinds_of_loops.shape[0]):
        found = jnp.where(slots >= loop_index * capacity, kinds_of_loops[loop_index], found)
    count = slots.shape[1]
    upto = lax.broadcasted_iota(jnp.int32, (count, count), 0) <= lax.broadcasted_iota(jnp.int32, (count, count), 1)
    upto = upto.astype(F32).astype(BF16)
    lane = lax.broadcasted_iota(jnp.int32, (1, count), 1).astype(F32)
    place = jnp.zeros((1, count), F32)
    kind = jnp.zeros((1, count), F32)
    start = jnp.zeros((1, 1), F32)
    for which in range(kinds):
        mine = (found == which).astype(F32)
        counted = jnp.dot(
            jnp.broadcast_to(mine, (8, count)).astype(BF16), upto, preferred_element_type=F32
        )[:1]
        place = place + mine * (start + counted - 1.0)
        if which:
            kind = kind + (lane >= start).astype(F32)
        start = start + jnp.sum(mine, axis=1, keepdims=True)
    places[...] = jnp.broadcast_to(place, places.shape)
    ordered = jnp.dot(placing(place), grads[...], preferred_element_type=F32).astype(BF16)
    cut = count // 2
    for part, out in enumerate((first, second)):
        extra = out.shape[0] - cut
        out[:cut] = ordered[part * cut:(part + 1) * cut]
        out[cut:] = jnp.zeros((extra, out.shape[1]), BF16)
        out[cut:, :cut] = jnp.broadcast_to(kind[:, part * cut:(part + 1) * cut], (extra, cut)).astype(BF16)


def packed_grads(out_grad, dest_row, loop_modality, capacity, kinds):
    rows, columns = out_grad.shape
    slots = dest_row.reshape(1, -1)
    packed = (rows // 2 + KIND_ROWS, columns)
    return pl.pallas_call(
        functools.partial(pack_kernel, capacity=capacity, kinds=kinds),
        grid_spec=pltpu.PrefetchScalarGridSpec(
            num_scalar_prefetch=1,
            grid=(1,),
            in_specs=[whole(slots.shape), whole(out_grad.shape)],
            out_specs=[whole(packed), whole(packed), whole((8, rows))],
        ),
        out_shape=[
            jax.ShapeDtypeStruct(packed, BF16), jax.ShapeDtypeStruct(packed, BF16), pltpu.HBM((8, rows), F32)
        ],
        compiler_params=limit(60),
    )(loop_modality, *in_hbm(slots, out_grad))


def sort_kernel(places, rows, out):
    out[...] = jnp.dot(placing(places[:1]), rows[...], preferred_element_type=F32).astype(BF16)


def sorted_rows(places, rows):
    return pl.pallas_call(
        sort_kernel,
        grid=(1,),
        in_specs=[whole(places.shape), whole(rows.shape)],
        out_specs=whole(rows.shape),
        out_shape=pltpu.HBM(rows.shape, BF16),
        compiler_params=limit(16),
    )(*in_hbm(places, rows))


def in_hbm(*values):
    return [pltpu.with_memory_space_constraint(value, pltpu.HBM) for value in values]


def kinds_in(refs):
    return jnp.concatenate([ref[:1].astype(F32) for ref in refs], axis=1)


def kind_spec(half_block):
    cut = half_block.shape[0] - KIND_ROWS
    return pl.BlockSpec((KIND_ROWS, cut), lambda *_: (cut // KIND_ROWS, 0))


def whole(shape):
    return pl.BlockSpec(shape, lambda *_: (0,) * len(shape))


def limit(mebibytes):
    return pltpu.CompilerParams(vmem_limit_bytes=mebibytes << 20)


def input_kernel(core, own_weight, other_weight, *refs, blocks, tile):
    cut = refs[0].shape[0] - KIND_ROWS
    halves = [refs[part:blocks:2] for part in (0, 1)]
    sides = [jnp.concatenate([ref[:cut] for ref in some], axis=0) for some in halves]
    kinds = [kinds_in([ref[cut:, :cut] for ref in some]) for some in halves]
    outs = refs[blocks:]
    half = outs[0].shape[1] // 2

    def product(weight, rows):
        return lax.dot_general(weight, rows, (((1,), (1,)), ((), ())), preferred_element_type=F32)

    for weight, side in ((own_weight, core[0]), (other_weight, 1 - core[0])):
        common = product(weight[1], jnp.concatenate(sides, axis=0))
        at = pl.multiple_of(side * half + pl.program_id(0) * tile, tile)
        span = sides[0].shape[0]
        for part, (special, _) in enumerate(PART_KINDS):
            mine = product(weight[special], sides[part])
            chosen = jnp.where(kinds[part] == special, mine, common[:, part * span:(part + 1) * span])
            chosen = chosen.astype(BF16).T
            for number, out in enumerate(outs):
                out[part * cut:(part + 1) * cut, pl.ds(at, tile)] = chosen[number * cut:(number + 1) * cut]


def input_terms(core, blocks, sizes, own_weight, other_weight):
    kinds, half, columns = own_weight.shape
    tile = min(half, 256)
    weight_spec = pl.BlockSpec((kinds, tile, columns), lambda step, core: (0, step, 0))
    return pl.pallas_call(
        functools.partial(input_kernel, blocks=len(blocks), tile=tile),
        grid_spec=pltpu.PrefetchScalarGridSpec(
            num_scalar_prefetch=1,
            grid=(half // tile,),
            in_specs=[weight_spec, weight_spec] + [whole(block.shape) for block in blocks],
            out_specs=[whole((size, 2 * half)) for size in sizes],
        ),
        out_shape=[pltpu.HBM((size, 2 * half), BF16) for size in sizes],
        compiler_params=limit(28),
    )(core, *in_hbm(own_weight, other_weight), *blocks)


def project_kernel(core, own_weight, other_weight, *refs, items):
    _, half, tile = own_weight.shape
    own_at = pl.multiple_of(core[0] * half, half)
    other_at = pl.multiple_of((1 - core[0]) * half, half)
    own = jnp.concatenate([ref[:, pl.ds(own_at, half)] for ref in refs[:items]], axis=0)
    other = jnp.concatenate([ref[:, pl.ds(other_at, half)] for ref in refs[:items]], axis=0)
    kind = kinds_in([ref[...] for ref in refs[items:2 * items]])
    row_kind = jnp.broadcast_to(kind, (tile, kind.shape[1])).T
    outs = refs[2 * items:]

    def product(which, rows):
        return (
            jnp.dot(own[rows], own_weight[which], preferred_element_type=F32)
            + jnp.dot(other[rows], other_weight[which], preferred_element_type=F32)
        )

    span = own.shape[0] // 2
    cut = outs[0].shape[0]
    common = product(1, slice(None))
    for part, (special, _) in enumerate(PART_KINDS):
        rows = slice(part * span, (part + 1) * span)
        chosen = jnp.where(row_kind[rows] == special, product(special, rows), common[rows]).astype(BF16)
        for number in range(items // 2):
            outs[part * (items // 2) + number][...] = chosen[number * cut:(number + 1) * cut]


def project_parts(core, items, own_weight, other_weight):
    kinds, half, columns = own_weight.shape
    tile = math.gcd(columns, PROJECT_TILE)
    weight_spec = pl.BlockSpec((kinds, half, tile), lambda step, core: (0, 0, step))
    cut = items[0][2].shape[0] - KIND_ROWS
    return pl.pallas_call(
        functools.partial(project_kernel, items=len(items)),
        grid_spec=pltpu.PrefetchScalarGridSpec(
            num_scalar_prefetch=1,
            grid=(columns // tile,),
            in_specs=[weight_spec, weight_spec]
            + [pl.BlockSpec((cut, 2 * half), lambda step, core, part=item[1]: (part, 0)) for item in items]
            + [kind_spec(item[2]) for item in items],
            out_specs=[pl.BlockSpec((cut, tile), lambda step, core: (0, step))] * len(items),
        ),
        out_shape=[pltpu.HBM((cut, columns), BF16)] * len(items),
        compiler_params=limit(28),
    )(core, *in_hbm(own_weight, other_weight), *[item[0] for item in items], *in_hbm(*[item[2] for item in items]))


def total_kernel(*refs, counts):
    outs = refs[sum(counts):]
    start = 0
    for count, out in zip(counts, outs):
        total = refs[start][...].astype(F32)
        for ref in refs[start + 1:start + count]:
            total = total + ref[...].astype(F32)
        out[...] = total.astype(BF16)
        start += count


def totals(groups):
    values = [value for group in groups for value in group]
    return pl.pallas_call(
        functools.partial(total_kernel, counts=[len(group) for group in groups]),
        grid=(1,),
        in_specs=[whole(value.shape) for value in values],
        out_specs=[whole(group[0].shape) for group in groups],
        out_shape=[pltpu.HBM(group[0].shape, BF16) for group in groups],
        compiler_params=limit(16),
    )(*in_hbm(*values))


def finish_kernel(places, term, *refs, count):
    projected, input_grad = refs[-2:]
    sums = []
    for part in (0, 1):
        total = refs[part * count][...].astype(F32)
        for ref in refs[part * count + 1:(part + 1) * count]:
            total = total + ref[...].astype(F32)
        sums.append(total.astype(BF16))
    back = placing(places[:1], F32).T.astype(BF16)
    projected[...] = jnp.dot(back, jnp.concatenate(sums, axis=0), preferred_element_type=F32).astype(BF16)
    input_grad[...] = jnp.dot(back, term[...], preferred_element_type=F32).astype(BF16)


def finish(places, term, first, second):
    cut, columns = first[0].shape
    shapes = ((2 * cut, columns), term.shape)
    return pl.pallas_call(
        functools.partial(finish_kernel, count=len(first)),
        grid=(1,),
        in_specs=[whole(places.shape), whole(term.shape)] + [whole((cut, columns))] * (2 * len(first)),
        out_specs=[whole(shape) for shape in shapes],
        out_shape=[jax.ShapeDtypeStruct(shape, BF16) for shape in shapes],
        compiler_params=limit(20),
    )(*in_hbm(places, term), *first, *second)


def fold_kernel(wanted, *refs, sources, counts):
    places = len(counts)
    added = refs[sources:sources + sum(counts)]
    outs = refs[sources + sum(counts):-2]
    held, done = refs[-2:]
    for place in range(places):
        for index in range(sources):
            @pl.when(wanted[place] == index)
            def _(place=place, index=index):
                pltpu.make_async_copy(refs[index], held.at[place], done.at[place]).start()
    start = 0
    for place, (count, out) in enumerate(zip(counts, outs)):
        pltpu.make_async_copy(refs[0], held.at[place], done.at[place]).wait()
        if count:
            total = held[place].astype(F32)
            for ref in added[start:start + count]:
                total = total + ref[...].astype(F32)
            out[...] = total.astype(BF16)
        else:
            out[...] = held[place]
        start += count


def fold(wanted, sources, groups):
    shape = sources[0].shape
    values = [value for group in groups for value in group]
    return pl.pallas_call(
        functools.partial(fold_kernel, sources=len(sources), counts=[len(group) for group in groups]),
        grid_spec=pltpu.PrefetchScalarGridSpec(
            num_scalar_prefetch=1,
            grid=(1,),
            in_specs=[pl.BlockSpec(memory_space=pl.ANY)] * len(sources) + [whole(shape)] * len(values),
            out_specs=[whole(shape)] * len(groups),
            scratch_shapes=[
                pltpu.VMEM((len(groups), *shape), BF16), pltpu.SemaphoreType.DMA((len(groups),))
            ],
        ),
        out_shape=[pltpu.HBM(shape, BF16)] * len(groups),
        compiler_params=limit(20),
    )(jnp.stack(wanted), *sources, *values)


def weight_kernel(core, *refs, blocks, grads, scale):
    rows = refs[:blocks]
    columns_of = refs[blocks:blocks + grads]
    kind_rows = refs[blocks + grads:blocks + 2 * grads]
    out, *turned = refs[blocks + 2 * grads:]

    @pl.when(pl.program_id(0) == 0)
    def _():
        for number, ref in enumerate(rows):
            cut = ref.shape[0] // 2
            block = ref[...].T
            for part, part_kinds in enumerate(PART_KINDS):
                own_kind = kind_rows[2 * number + part][:1].astype(F32)
                for place, which in enumerate(part_kinds):
                    turned[part][place, :, number * cut:(number + 1) * cut] = jnp.where(
                        own_kind == which, block[:, part * cut:(part + 1) * cut], 0
                    )

    columns = [jnp.concatenate([ref[...] for ref in columns_of[part::2]], axis=0) for part in (0, 1)]
    common = sum(jnp.dot(turned[part][1], columns[part], preferred_element_type=F32) for part in (0, 1))
    out[1] = (common * scale).astype(BF16)
    for part, (special, _) in enumerate(PART_KINDS):
        total = jnp.dot(turned[part][0], columns[part], preferred_element_type=F32)
        out[special] = (total * scale).astype(BF16)


def weight_gradient(core, blocks, half_blocks, kinds, scale):
    rows, features = blocks[0].shape
    half = features // 2
    columns = half_blocks[0].shape[1]
    cut = half_blocks[0].shape[0] - KIND_ROWS
    tile = math.gcd(columns, WEIGHT_TILE)
    return pl.pallas_call(
        functools.partial(weight_kernel, blocks=len(blocks), grads=len(half_blocks), scale=scale),
        grid_spec=pltpu.PrefetchScalarGridSpec(
            num_scalar_prefetch=1,
            grid=(columns // tile,),
            in_specs=[pl.BlockSpec((rows, half), lambda step, core: (0, core[0])) for _ in blocks]
            + [pl.BlockSpec((cut, tile), lambda step, core: (0, step)) for _ in half_blocks]
            + [kind_spec(block) for block in half_blocks],
            out_specs=pl.BlockSpec((kinds, half, tile), lambda step, core: (0, 0, step)),
            scratch_shapes=[pltpu.VMEM((2, half, rows // 2 * len(blocks)), BF16)] * 2,
        ),
        out_shape=jax.ShapeDtypeStruct((kinds, half, columns), BF16),
        compiler_params=limit(36),
    )(core, *in_hbm(*blocks, *half_blocks, *half_blocks))


def low_high(offset):
    return offset & -offset, 1 << (offset.bit_length() - 1)


def body(tokens, out_grad, qkv_weight, dest_row, loop_modality):
    loop_count = lax.axis_size("loop")
    tp_count = lax.axis_size("tp")
    row_count, feature_part = tokens.shape
    kinds, half, _ = qkv_weight.shape
    chip_count = loop_count // 2
    assert chip_count == tp_count and 2 * half == feature_part
    capacity = 3 * row_count // (2 * loop_count)
    grad_scale = 1.0 / math.sqrt(row_count * loop_count)
    loop_index = lax.axis_index("loop")
    chip, level = loop_index >> 1, lax.axis_index("tp")
    core = (loop_index & 1).reshape(1)
    bits = [1 << place for place in range(chip_count.bit_length() - 1)]
    offsets = sorted(range(1, chip_count), key=lambda offset: (bin(offset).count("1"), offset))
    several = [offset for offset in offsets if offset & (offset - 1)]
    cut = row_count // 2

    def across(value, offset):
        pairs = [(i, i ^ (2 * offset)) for i in range(loop_count)]
        return lax.ppermute(value, "loop", pairs)

    def sibling(value):
        return lax.ppermute(value, "loop", [(i, i ^ 1) for i in range(loop_count)])

    def line_pairs(parity, stage):
        pairs = []
        for low in range(parity, tp_count - 1, 2):
            if low - stage + 1 >= 0:
                pairs.append((low, low + 1))
            if low + stage <= tp_count - 1:
                pairs.append((low + 1, low))
        return pairs

    def along(value, pairs):
        return lax.ppermute(value, "tp", pairs)

    stages = range(1, tp_count)
    facing = [jnp.where(level % 2 == parity, 1, -1) for parity in (0, 1)]

    assert kinds == 3 and capacity * loop_count // 4 <= cut
    other_weight = sibling(qkv_weight)
    *own_grad, order = packed_grads(out_grad, dest_row, loop_modality, capacity, kinds)
    tokens = sorted_rows(order, tokens)
    came = {(0, 0): tokens, (1, 0): tokens}
    for stage in stages:
        for parity in (0, 1):
            pairs = line_pairs(parity, stage)
            if pairs:
                came[parity, stage] = along(came[1 - parity, stage - 1], pairs)

    grads = {0: own_grad}
    for bit in bits:
        grads[bit] = [None, None]
    for bit in bits:
        first = 0 if bit == bits[-1] else 1
        for part in (first, 1 - first):
            grads[bit][part] = across(own_grad[part], bit)
    for offset in several:
        low, high = low_high(offset)
        grads[offset] = [across(grads[offset ^ low][0], low), across(grads[offset ^ high][1], high)]

    def halves_of(group):
        return [part for offset in group for part in grads[offset]]

    arrived = {}
    for group in ([0], bits, several):
        blocks = halves_of(group)
        made = input_terms(
            core, blocks if group == several else in_hbm(*blocks), [row_count] * len(group), qkv_weight, other_weight
        )
        for offset, term in zip(group, made):
            arrived[offset] = across(term, offset) if offset else term
    all_terms = in_hbm(*[arrived[offset] for offset in range(chip_count)])

    def term_number(where):
        return chip ^ jnp.clip(where, 0, tp_count - 1)

    back = {}
    for stage in reversed(stages):
        links = [parity for parity in (0, 1) if line_pairs(parity, stage)]
        wanted = [term_number(level + stage * facing[parity]) for parity in links]
        groups = [[back[1 - parity, stage + 1]] if (1 - parity, stage + 1) in back else [] for parity in links]
        made = fold(wanted, all_terms, groups)
        for parity, value in zip(links, made):
            pairs = [(b, a) for a, b in line_pairs(parity, stage)]
            back[parity, stage] = along(value, pairs)
    last = [back[parity, 1] for parity in (0, 1) if (parity, 1) in back]
    own_input = fold([term_number(level)], all_terms, [last])[0]

    places = [place for place in came if place != (1, 0)]
    sources = [came[place] for place in places]
    wanted = []
    for offset in range(chip_count):
        where = chip ^ offset
        index = jnp.int32(0)
        for number, (parity, stage) in enumerate(places):
            if stage:
                index = jnp.where(where == level + stage * facing[parity], number, index)
        wanted.append(index)
    sends = fold(wanted, in_hbm(*sources), [[]] * chip_count)
    rows = {offset: across(sends[offset], offset) if offset else sends[offset] for offset in range(chip_count)}

    pieces = {(offset, part): [] for offset in range(chip_count) for part in (0, 1)}

    def project(places):
        places = sorted(places, key=lambda place: place[1])
        items = [(rows[offset], part, grads[offset][part]) for offset, part in places]
        made = project_parts(core, items, qkv_weight, other_weight)
        return dict(zip(places, made))

    own_parts = project([(0, 0), (0, 1)])
    for weight in range(len(bits), 0, -1):
        places = [(offset, part) for offset in offsets if bin(offset).count("1") == weight for part in (0, 1)]
        made = project(places)
        summed = [place for place in places if pieces[place]]
        if summed:
            sums = totals([[made[place], *pieces[place]] for place in summed])
            made.update(zip(summed, sums))
        for offset, part in places:
            link = offset if offset in bits else low_high(offset)[part]
            piece = across(made[offset, part], link)
            pieces[offset ^ link, part].append(piece)
    projected, input_grad = finish(order, own_input, [own_parts[0, 0], *pieces[0, 0]], [own_parts[0, 1], *pieces[0, 1]])

    near = [rows[offset] for offset in range(chip_count)]
    far = [sibling(block) for block in near]
    near_grads = halves_of(range(chip_count))
    far_grads = [sibling(block) for block in near_grads]
    weight_grad = weight_gradient(core, near + far, near_grads + far_grads, kinds, grad_scale)
    return projected, input_grad, weight_grad


def solution(mesh):
    placed = (P("loop", "tp"), P("loop", "tp"), P(None, "loop", "tp"), P("loop"), P())
    return jax.shard_map(
        body,
        mesh=mesh,
        in_specs=placed,
        out_specs=(P("loop", "tp"), P("loop", "tp"), P(None, "loop", "tp")),
        check_vma=False,
    )
```

```python
import functools
import math

import jax
import jax.numpy as jnp
from jax import lax
from jax.experimental import pallas as pl
from jax.experimental.pallas import tpu as pltpu
from jax.sharding import PartitionSpec as P


BF16 = jnp.bfloat16
F32 = jnp.float32
KIND_ROWS = 8
PART_KINDS = ((0, 1), (2, 1))
PROJECT_TILE = 512
SMALL_PROJECT_TILE = 768
WEIGHT_TILE = 512


def placing(place, dtype=BF16):
    count = place.shape[1]
    rows = lax.broadcasted_iota(jnp.int32, (count, count), 0)
    return (rows == place.astype(jnp.int32)).astype(F32).astype(dtype)


def pack_kernel(kinds_of_loops, dest, grads, first, second, places, *, capacity, kinds):
    slots = dest[...]
    found = jnp.full(slots.shape, kinds_of_loops[0], jnp.int32)
    for loop_index in range(1, kinds_of_loops.shape[0]):
        found = jnp.where(slots >= loop_index * capacity, kinds_of_loops[loop_index], found)
    count = slots.shape[1]
    upto = lax.broadcasted_iota(jnp.int32, (count, count), 0) <= lax.broadcasted_iota(jnp.int32, (count, count), 1)
    upto = upto.astype(F32).astype(BF16)
    lane = lax.broadcasted_iota(jnp.int32, (1, count), 1).astype(F32)
    place = jnp.zeros((1, count), F32)
    kind = jnp.zeros((1, count), F32)
    start = jnp.zeros((1, 1), F32)
    for which in range(kinds):
        mine = (found == which).astype(F32)
        counted = jnp.dot(
            jnp.broadcast_to(mine, (8, count)).astype(BF16), upto, preferred_element_type=F32
        )[:1]
        place = place + mine * (start + counted - 1.0)
        if which:
            kind = kind + (lane >= start).astype(F32)
        start = start + jnp.sum(mine, axis=1, keepdims=True)
    places[...] = jnp.broadcast_to(place, places.shape)
    ordered = jnp.dot(placing(place), grads[...], preferred_element_type=F32).astype(BF16)
    cut = count // 2
    for part, out in enumerate((first, second)):
        extra = out.shape[0] - cut
        out[:cut] = ordered[part * cut:(part + 1) * cut]
        out[cut:] = jnp.zeros((extra, out.shape[1]), BF16)
        out[cut:, :cut] = jnp.broadcast_to(kind[:, part * cut:(part + 1) * cut], (extra, cut)).astype(BF16)


def packed_grads(out_grad, dest_row, loop_modality, capacity, kinds):
    rows, columns = out_grad.shape
    slots = dest_row.reshape(1, -1)
    packed = (rows // 2 + KIND_ROWS, columns)
    return pl.pallas_call(
        functools.partial(pack_kernel, capacity=capacity, kinds=kinds),
        grid_spec=pltpu.PrefetchScalarGridSpec(
            num_scalar_prefetch=1,
            grid=(1,),
            in_specs=[whole(slots.shape), whole(out_grad.shape)],
            out_specs=[whole(packed), whole(packed), whole((8, rows))],
        ),
        out_shape=[
            jax.ShapeDtypeStruct(packed, BF16), jax.ShapeDtypeStruct(packed, BF16), pltpu.HBM((8, rows), F32)
        ],
        compiler_params=limit(60),
    )(loop_modality, *in_hbm(slots, out_grad))


def sort_kernel(places, rows, out):
    out[...] = jnp.dot(placing(places[:1]), rows[...], preferred_element_type=F32).astype(BF16)


def sorted_rows(places, rows):
    return pl.pallas_call(
        sort_kernel,
        grid=(1,),
        in_specs=[whole(places.shape), whole(rows.shape)],
        out_specs=whole(rows.shape),
        out_shape=pltpu.HBM(rows.shape, BF16),
        compiler_params=limit(16),
    )(*in_hbm(places, rows))


def in_hbm(*values):
    return [pltpu.with_memory_space_constraint(value, pltpu.HBM) for value in values]


def kinds_in(refs):
    return jnp.concatenate([ref[:1].astype(F32) for ref in refs], axis=1)


def kind_spec(half_block):
    cut = half_block.shape[0] - KIND_ROWS
    return pl.BlockSpec((KIND_ROWS, cut), lambda *_: (cut // KIND_ROWS, 0))


def whole(shape):
    return pl.BlockSpec(shape, lambda *_: (0,) * len(shape))


def limit(mebibytes):
    return pltpu.CompilerParams(vmem_limit_bytes=mebibytes << 20)


def input_kernel(core, own_weight, other_weight, *refs, blocks, tile):
    cut = refs[0].shape[0] - KIND_ROWS
    halves = [refs[part:blocks:2] for part in (0, 1)]
    sides = [jnp.concatenate([ref[:cut] for ref in some], axis=0) for some in halves]
    kinds = [kinds_in([ref[cut:, :cut] for ref in some]) for some in halves]
    outs = refs[blocks:]
    half = outs[0].shape[1] // 2

    def product(weight, rows):
        return lax.dot_general(weight, rows, (((1,), (1,)), ((), ())), preferred_element_type=F32)

    for weight, side in ((own_weight, core[0]), (other_weight, 1 - core[0])):
        common = product(weight[1], jnp.concatenate(sides, axis=0))
        at = pl.multiple_of(side * half + pl.program_id(0) * tile, tile)
        span = sides[0].shape[0]
        for part, (special, _) in enumerate(PART_KINDS):
            mine = product(weight[special], sides[part])
            chosen = jnp.where(kinds[part] == special, mine, common[:, part * span:(part + 1) * span])
            chosen = chosen.astype(BF16).T
            for number, out in enumerate(outs):
                out[part * cut:(part + 1) * cut, pl.ds(at, tile)] = chosen[number * cut:(number + 1) * cut]


def input_terms(core, blocks, sizes, own_weight, other_weight):
    kinds, half, columns = own_weight.shape
    tile = min(half, 256)
    weight_spec = pl.BlockSpec((kinds, tile, columns), lambda step, core: (0, step, 0))
    return pl.pallas_call(
        functools.partial(input_kernel, blocks=len(blocks), tile=tile),
        grid_spec=pltpu.PrefetchScalarGridSpec(
            num_scalar_prefetch=1,
            grid=(half // tile,),
            in_specs=[weight_spec, weight_spec] + [whole(block.shape) for block in blocks],
            out_specs=[whole((size, 2 * half)) for size in sizes],
        ),
        out_shape=[pltpu.HBM((size, 2 * half), BF16) for size in sizes],
        compiler_params=limit(28),
    )(core, *in_hbm(own_weight, other_weight), *blocks)


def project_kernel(core, own_weight, other_weight, *refs, items):
    _, half, tile = own_weight.shape
    own_at = pl.multiple_of(core[0] * half, half)
    other_at = pl.multiple_of((1 - core[0]) * half, half)
    own = jnp.concatenate([ref[:, pl.ds(own_at, half)] for ref in refs[:items]], axis=0)
    other = jnp.concatenate([ref[:, pl.ds(other_at, half)] for ref in refs[:items]], axis=0)
    kind = kinds_in([ref[...] for ref in refs[items:2 * items]])
    row_kind = jnp.broadcast_to(kind, (tile, kind.shape[1])).T
    outs = refs[2 * items:]

    def product(which, rows):
        return (
            jnp.dot(own[rows], own_weight[which], preferred_element_type=F32)
            + jnp.dot(other[rows], other_weight[which], preferred_element_type=F32)
        )

    span = own.shape[0] // 2
    cut = outs[0].shape[0]
    common = product(1, slice(None))
    for part, (special, _) in enumerate(PART_KINDS):
        rows = slice(part * span, (part + 1) * span)
        chosen = jnp.where(row_kind[rows] == special, product(special, rows), common[rows]).astype(BF16)
        for number in range(items // 2):
            outs[part * (items // 2) + number][...] = chosen[number * cut:(number + 1) * cut]


def project_parts(core, items, own_weight, other_weight):
    kinds, half, columns = own_weight.shape
    tile = math.gcd(columns, PROJECT_TILE if len(items) > 2 else SMALL_PROJECT_TILE)
    weight_spec = pl.BlockSpec((kinds, half, tile), lambda step, core: (0, 0, step))
    cut = items[0][2].shape[0] - KIND_ROWS
    return pl.pallas_call(
        functools.partial(project_kernel, items=len(items)),
        grid_spec=pltpu.PrefetchScalarGridSpec(
            num_scalar_prefetch=1,
            grid=(columns // tile,),
            in_specs=[weight_spec, weight_spec]
            + [pl.BlockSpec((cut, 2 * half), lambda step, core, part=item[1]: (part, 0)) for item in items]
            + [kind_spec(item[2]) for item in items],
            out_specs=[pl.BlockSpec((cut, tile), lambda step, core: (0, step))] * len(items),
        ),
        out_shape=[pltpu.HBM((cut, columns), BF16)] * len(items),
        compiler_params=limit(28),
    )(core, *in_hbm(own_weight, other_weight, *[item[0] for item in items], *[item[2] for item in items]))


def total_kernel(*refs, counts):
    outs = refs[sum(counts):]
    start = 0
    for count, out in zip(counts, outs):
        total = refs[start][...].astype(F32)
        for ref in refs[start + 1:start + count]:
            total = total + ref[...].astype(F32)
        out[...] = total.astype(BF16)
        start += count


def totals(groups):
    values = [value for group in groups for value in group]
    return pl.pallas_call(
        functools.partial(total_kernel, counts=[len(group) for group in groups]),
        grid=(1,),
        in_specs=[whole(value.shape) for value in values],
        out_specs=[whole(group[0].shape) for group in groups],
        out_shape=[pltpu.HBM(group[0].shape, BF16) for group in groups],
        compiler_params=limit(16),
    )(*in_hbm(*values))


def finish_kernel(places, term, *refs, count):
    projected, input_grad = refs[-2:]
    sums = []
    for part in (0, 1):
        total = refs[part * count][...].astype(F32)
        for ref in refs[part * count + 1:(part + 1) * count]:
            total = total + ref[...].astype(F32)
        sums.append(total.astype(BF16))
    back = placing(places[:1], F32).T.astype(BF16)
    projected[...] = jnp.dot(back, jnp.concatenate(sums, axis=0), preferred_element_type=F32).astype(BF16)
    input_grad[...] = jnp.dot(back, term[...], preferred_element_type=F32).astype(BF16)


def finish(places, term, first, second):
    cut, columns = first[0].shape
    shapes = ((2 * cut, columns), term.shape)
    return pl.pallas_call(
        functools.partial(finish_kernel, count=len(first)),
        grid=(1,),
        in_specs=[whole(places.shape), whole(term.shape)] + [whole((cut, columns))] * (2 * len(first)),
        out_specs=[whole(shape) for shape in shapes],
        out_shape=[jax.ShapeDtypeStruct(shape, BF16) for shape in shapes],
        compiler_params=limit(20),
    )(*in_hbm(places, term), *first, *second)


def fold_kernel(wanted, *refs, sources, counts):
    places = len(counts)
    added = refs[sources:sources + sum(counts)]
    outs = refs[sources + sum(counts):-2]
    held, done = refs[-2:]
    for place in range(places):
        for index in range(sources):
            @pl.when(wanted[place] == index)
            def _(place=place, index=index):
                pltpu.make_async_copy(refs[index], held.at[place], done.at[place]).start()
    start = 0
    for place, (count, out) in enumerate(zip(counts, outs)):
        pltpu.make_async_copy(refs[0], held.at[place], done.at[place]).wait()
        if count:
            total = held[place].astype(F32)
            for ref in added[start:start + count]:
                total = total + ref[...].astype(F32)
            out[...] = total.astype(BF16)
        else:
            out[...] = held[place]
        start += count


def fold(wanted, sources, groups):
    shape = sources[0].shape
    values = [value for group in groups for value in group]
    return pl.pallas_call(
        functools.partial(fold_kernel, sources=len(sources), counts=[len(group) for group in groups]),
        grid_spec=pltpu.PrefetchScalarGridSpec(
            num_scalar_prefetch=1,
            grid=(1,),
            in_specs=[pl.BlockSpec(memory_space=pl.ANY)] * len(sources) + [whole(shape)] * len(values),
            out_specs=[whole(shape)] * len(groups),
            scratch_shapes=[
                pltpu.VMEM((len(groups), *shape), BF16), pltpu.SemaphoreType.DMA((len(groups),))
            ],
        ),
        out_shape=[pltpu.HBM(shape, BF16)] * len(groups),
        compiler_params=limit(20),
    )(jnp.stack(wanted), *sources, *values)


def weight_kernel(core, *refs, blocks, grads, scale):
    rows = refs[:blocks]
    columns_of = refs[blocks:blocks + grads]
    kind_rows = refs[blocks + grads:blocks + 2 * grads]
    out, *turned = refs[blocks + 2 * grads:]

    @pl.when(pl.program_id(0) == 0)
    def _():
        for number, ref in enumerate(rows):
            cut = ref.shape[0] // 2
            block = ref[...].T
            for part, part_kinds in enumerate(PART_KINDS):
                own_kind = kind_rows[2 * number + part][:1].astype(F32)
                for place, which in enumerate(part_kinds):
                    turned[part][place, :, number * cut:(number + 1) * cut] = jnp.where(
                        own_kind == which, block[:, part * cut:(part + 1) * cut], 0
                    )

    columns = [jnp.concatenate([ref[...] for ref in columns_of[part::2]], axis=0) for part in (0, 1)]
    common = sum(jnp.dot(turned[part][1], columns[part], preferred_element_type=F32) for part in (0, 1))
    out[1] = (common * scale).astype(BF16)
    for part, (special, _) in enumerate(PART_KINDS):
        total = jnp.dot(turned[part][0], columns[part], preferred_element_type=F32)
        out[special] = (total * scale).astype(BF16)


def weight_gradient(core, blocks, half_blocks, kinds, scale):
    rows, features = blocks[0].shape
    half = features // 2
    columns = half_blocks[0].shape[1]
    cut = half_blocks[0].shape[0] - KIND_ROWS
    tile = math.gcd(columns, WEIGHT_TILE)
    return pl.pallas_call(
        functools.partial(weight_kernel, blocks=len(blocks), grads=len(half_blocks), scale=scale),
        grid_spec=pltpu.PrefetchScalarGridSpec(
            num_scalar_prefetch=1,
            grid=(columns // tile,),
            in_specs=[pl.BlockSpec((rows, half), lambda step, core: (0, core[0])) for _ in blocks]
            + [pl.BlockSpec((cut, tile), lambda step, core: (0, step)) for _ in half_blocks]
            + [kind_spec(block) for block in half_blocks],
            out_specs=pl.BlockSpec((kinds, half, tile), lambda step, core: (0, 0, step)),
            scratch_shapes=[pltpu.VMEM((2, half, rows // 2 * len(blocks)), BF16)] * 2,
        ),
        out_shape=jax.ShapeDtypeStruct((kinds, half, columns), BF16),
        compiler_params=limit(36),
    )(core, *in_hbm(*blocks, *half_blocks, *half_blocks))


def low_high(offset):
    return offset & -offset, 1 << (offset.bit_length() - 1)


def body(tokens, out_grad, qkv_weight, dest_row, loop_modality):
    loop_count = lax.axis_size("loop")
    tp_count = lax.axis_size("tp")
    row_count, feature_part = tokens.shape
    kinds, half, _ = qkv_weight.shape
    chip_count = loop_count // 2
    assert chip_count == tp_count and 2 * half == feature_part
    capacity = 3 * row_count // (2 * loop_count)
    grad_scale = 1.0 / math.sqrt(row_count * loop_count)
    loop_index = lax.axis_index("loop")
    chip, level = loop_index >> 1, lax.axis_index("tp")
    core = (loop_index & 1).reshape(1)
    bits = [1 << place for place in range(chip_count.bit_length() - 1)]
    offsets = sorted(range(1, chip_count), key=lambda offset: (bin(offset).count("1"), offset))
    several = [offset for offset in offsets if offset & (offset - 1)]
    cut = row_count // 2

    def across(value, offset):
        pairs = [(i, i ^ (2 * offset)) for i in range(loop_count)]
        return lax.ppermute(value, "loop", pairs)

    def sibling(value):
        return lax.ppermute(value, "loop", [(i, i ^ 1) for i in range(loop_count)])

    def line_pairs(parity, stage):
        pairs = []
        for low in range(parity, tp_count - 1, 2):
            if low - stage + 1 >= 0:
                pairs.append((low, low + 1))
            if low + stage <= tp_count - 1:
                pairs.append((low + 1, low))
        return pairs

    def along(value, pairs):
        return lax.ppermute(value, "tp", pairs)

    stages = range(1, tp_count)
    facing = [jnp.where(level % 2 == parity, 1, -1) for parity in (0, 1)]

    assert kinds == 3 and capacity * loop_count // 4 <= cut
    other_weight = sibling(qkv_weight)
    *own_grad, order = packed_grads(out_grad, dest_row, loop_modality, capacity, kinds)
    tokens = sorted_rows(order, tokens)
    came = {(0, 0): tokens, (1, 0): tokens}
    for stage in stages:
        for parity in (0, 1):
            pairs = line_pairs(parity, stage)
            if pairs:
                came[parity, stage] = along(came[1 - parity, stage - 1], pairs)

    grads = {0: own_grad}
    for bit in bits:
        grads[bit] = [None, None]
    for bit in bits:
        first = 0 if bit == bits[-1] else 1
        for part in (first, 1 - first):
            grads[bit][part] = across(own_grad[part], bit)
    for offset in several:
        low, high = low_high(offset)
        grads[offset] = [across(grads[offset ^ low][0], low), across(grads[offset ^ high][1], high)]

    def halves_of(group):
        return [part for offset in group for part in grads[offset]]

    arrived = {}
    for group in ([0], bits, several):
        blocks = halves_of(group)
        made = input_terms(
            core, blocks if group == several else in_hbm(*blocks), [row_count] * len(group), qkv_weight, other_weight
        )
        for offset, term in zip(group, made):
            arrived[offset] = across(term, offset) if offset else term
    all_terms = [arrived[offset] for offset in range(chip_count)]

    def term_number(where):
        return chip ^ jnp.clip(where, 0, tp_count - 1)

    back = {}
    for stage in reversed(stages):
        links = [parity for parity in (0, 1) if line_pairs(parity, stage)]
        wanted = [term_number(level + stage * facing[parity]) for parity in links]
        groups = [[back[1 - parity, stage + 1]] if (1 - parity, stage + 1) in back else [] for parity in links]
        made = fold(wanted, all_terms, groups)
        for parity, value in zip(links, made):
            pairs = [(b, a) for a, b in line_pairs(parity, stage)]
            back[parity, stage] = along(value, pairs)
    last = [back[parity, 1] for parity in (0, 1) if (parity, 1) in back]
    own_input = fold([term_number(level)], all_terms, [last])[0]

    places = [place for place in came if place != (1, 0)]
    sources = [came[place] for place in places]
    wanted = []
    for offset in range(chip_count):
        where = chip ^ offset
        index = jnp.int32(0)
        for number, (parity, stage) in enumerate(places):
            if stage:
                index = jnp.where(where == level + stage * facing[parity], number, index)
        wanted.append(index)
    sends = fold(wanted, in_hbm(*sources), [[]] * chip_count)
    rows = {offset: across(sends[offset], offset) if offset else sends[offset] for offset in range(chip_count)}

    pieces = {(offset, part): [] for offset in range(chip_count) for part in (0, 1)}

    def project(places):
        places = sorted(places, key=lambda place: place[1])
        items = [(rows[offset], part, grads[offset][part]) for offset, part in places]
        made = project_parts(core, items, qkv_weight, other_weight)
        return dict(zip(places, made))

    own_parts = project([(0, 0), (0, 1)])
    for weight in range(len(bits), 0, -1):
        places = [(offset, part) for offset in offsets if bin(offset).count("1") == weight for part in (0, 1)]
        made = project(places)
        summed = [place for place in places if pieces[place]]
        if summed:
            sums = totals([[made[place], *pieces[place]] for place in summed])
            made.update(zip(summed, sums))
        for offset, part in places:
            link = offset if offset in bits else low_high(offset)[part]
            piece = across(made[offset, part], link)
            pieces[offset ^ link, part].append(piece)
    projected, input_grad = finish(order, own_input, [own_parts[0, 0], *pieces[0, 0]], [own_parts[0, 1], *pieces[0, 1]])

    near = [rows[offset] for offset in range(chip_count)]
    far = [sibling(block) for block in near]
    near_grads = halves_of(range(chip_count))
    far_grads = [sibling(block) for block in near_grads]
    weight_grad = weight_gradient(core, near + far, near_grads + far_grads, kinds, grad_scale)
    return projected, input_grad, weight_grad


def solution(mesh):
    placed = (P("loop", "tp"), P("loop", "tp"), P(None, "loop", "tp"), P("loop"), P())
    return jax.shard_map(
        body,
        mesh=mesh,
        in_specs=placed,
        out_specs=(P("loop", "tp"), P("loop", "tp"), P(None, "loop", "tp")),
        check_vma=False,
    )
```
